32 devices in a mesh: groups: 2 (over y), seq: 4 (over z), hid: 2 (over x), sub: 2 (over core).
Axes of the slice: x: 2, y: 2, z: 4, core: 2. Of those that a mesh axis runs over, the one named last changes fastest.
Arguments:
- z_mix: bfloat16 [16384, 768], P(('groups', 'seq', 'sub')), parts along dimension 0, may hold values from -6 to 6
- z_ffn: bfloat16 [16384, 768], P(('groups', 'seq', 'sub')), parts along dimension 0, may hold values from -6 to 6
- pre_act: bfloat16 [16384, 3072], P(('groups', 'seq', 'sub'), 'hid'), parts along dimension 0, may hold values from -6 to 6
- grad_out: bfloat16 [16384, 768], P(('groups', 'seq', 'sub')), parts along dimension 0, may hold values from -6 to 6
- gain_mix: float32 [768], replicated, may hold values from 0.1 to 1.9
- gain_ffn: float32 [768], replicated, may hold values from 0.1 to 1.9
- w_in: bfloat16 [768, 3072], P(('seq', 'sub'), 'hid'), may hold values from -0.21875 to 0.21875
- w_out: bfloat16 [768, 3072], P(('seq', 'sub'), 'hid'), may hold values from -0.109375 to 0.109375
Outputs:
- grad_in: float32 [16384, 768], P(('groups', 'seq', 'sub'), 'hid'), parts along dimension 0
- grad_w_in: float32 [1536, 3072], P(('groups', 'seq', 'sub'), 'hid'), parts along dimension 0
- grad_w_out: float32 [1536, 3072], P(('groups', 'seq', 'sub'), 'hid'), parts along dimension 0
The draws below stay inside these ranges and needn't reach their ends.
There are 2 independent parts, one for each index of `groups`. The reference program is written for one: setup_inputs(seed, part) draws one part's arguments, and reference() takes and returns one part's arrays. A program takes and returns all parts, laid end to end along the dimension named above; an argument that names none is the same for every part. Nothing has to cross between parts.
All inputs are finite; a program needn't handle non-finite values.
Results may differ from the reference program's by a relative error of at most 0.014.
Values may be sent and summed in bfloat16 or wider, within the bound.
No kernel may reach another device: no remote copies, remote signals or barrier semaphores. Data moves between devices by JAX's collectives and lax.ppermute only.
A program may use at most 64 MiB of HBM per device.

```python
import math
import jax
import jax.numpy as jnp
from jax import lax

D = 768
FF = 3072
TOKENS = 8192
N_HID = 2


def spiked(entries, own_key, source, target, parts, factor):
    def block_of(axis_at):
        return (jnp.arange(entries.shape[axis_at]) // (entries.shape[axis_at] // parts)).reshape((-1,) + (1,) * (entries.ndim - 1 - axis_at))

    first = jax.random.permutation(own_key, parts)[block_of(target)]
    far = (block_of(target) + parts // 2) % parts
    return jnp.where((block_of(source) == first) | (block_of(source) == far), factor * entries, entries)


def block_levels(stream_key, shape, split, least, largest):
    factor_of, own = 1.0, jax.random.fold_in(stream_key, 6)
    for axis_at, blocks in split:
        draws = jnp.exp(jax.random.uniform(jax.random.fold_in(own, axis_at), (blocks,), jnp.float32, least / len(split), largest / len(split)))
        factor_of = factor_of * jnp.repeat(draws, shape[axis_at] // blocks).reshape([-1 if axis == axis_at else 1 for axis in range(len(shape))])
    return factor_of


def gaussian(rng, extent, width, bound, split=(), kind=jnp.bfloat16):
    loudness = block_levels(rng, extent, split, -0.22, 0.18) if split else 1.0
    entries = jax.random.normal(rng, extent, jnp.float32) * width * loudness
    return jnp.minimum(jnp.maximum(entries, -bound), bound).astype(kind)


def bell_draw_with(stream_key, extent, spread, reach, shards, heavy, held_as=jnp.bfloat16):
    drawn = spread * jax.random.normal(stream_key, extent, jnp.float32)
    if shards:
        drawn = drawn * block_levels(stream_key, extent, shards, -0.22, 0.18)
    return jnp.clip(spiked(drawn, jax.random.fold_in(stream_key, 3), *heavy), -reach, reach).astype(held_as)


def setup_inputs(seed: int = 0, part: int = 0) -> dict:
    keys = jax.random.split(jax.random.key(seed), 9)
    part_splits = jax.random.split(jax.random.fold_in(keys[8], part), 9)
    z_mix = gaussian(part_splits[0], (TOKENS, D), 1.0, 6.0, ((0, 8),))
    z_ffn = gaussian(part_splits[1], (TOKENS, D), 1.0, 6.0, ((0, 8),))
    pre_act = gaussian(part_splits[2], (TOKENS, FF), 1.0, 6.0, ((0, 8), (1, 2)))
    grad_out = bell_draw_with(part_splits[3], (TOKENS, D), 1.0, 6.0, ((0, 8),), (0, 1, 8, 2.0))
    gain_mix = jnp.clip(1.0 + 0.18 * jax.random.normal(keys[4], (D,), jnp.float32), 0.1, 1.9)
    gain_ffn = jnp.clip(1.0 + 0.18 * jax.random.normal(keys[5], (D,), jnp.float32), 0.1, 1.9)
    w_in = gaussian(keys[6], (D, FF), D ** -0.5, 0.21875, ((0, 8), (1, 2)))
    w_out = gaussian(keys[7], (D, FF), FF ** -0.5, 0.109375, ((0, 8), (1, 2)))
    return dict(z_mix=z_mix, z_ffn=z_ffn, pre_act=pre_act, grad_out=grad_out, gain_mix=gain_mix, gain_ffn=gain_ffn, w_in=w_in, w_out=w_out)


epsilon = 1e-05

def norm_parts(values):
    values = values.astype(jnp.float32)
    row_mean = lax.optimization_barrier(jnp.mean(values, axis=-1, keepdims=True))
    centred = values - row_mean
    inv_std = lax.rsqrt(lax.optimization_barrier(jnp.mean(centred * centred, axis=-1, keepdims=True)) + epsilon)
    return (centred * inv_std, inv_std)

def norm_backward(values, gain_vec, upstream):
    unit_rows, inv_std = norm_parts(values)
    scaled = upstream * gain_vec
    return inv_std * (scaled - lax.optimization_barrier(jnp.mean(scaled, axis=-1, keepdims=True)) - unit_rows * lax.optimization_barrier(jnp.mean(scaled * unit_rows, axis=-1, keepdims=True)))

def gelu_tanh(values):
    return jax.nn.gelu(values, approximate=True)

def reference(z_mix, z_ffn, pre_act, grad_out, gain_mix, gain_ffn, w_in, w_out):
    normed = (norm_parts(z_mix)[0] * gain_mix).astype(jnp.bfloat16)
    ffn_grad = norm_backward(z_ffn, gain_ffn, grad_out.astype(jnp.float32))
    ffn_low = ffn_grad.astype(jnp.bfloat16)
    pre_wide = pre_act.astype(jnp.float32)
    activation = gelu_tanh(pre_wide).astype(jnp.bfloat16)
    act_grad = jnp.dot(ffn_low, w_out, preferred_element_type=jnp.float32)
    _, pull_back = jax.vjp(gelu_tanh, pre_wide)
    pre_grad = pull_back(act_grad)[0].astype(jnp.bfloat16)
    grad_w_in = jnp.dot(normed.T, pre_grad, preferred_element_type=jnp.float32)
    grad_w_out = jnp.dot(ffn_low.T, activation, preferred_element_type=jnp.float32)
    block_units = FF // N_HID

    def add_block(running, block_id):
        offset = block_id * block_units
        grad_block = lax.dynamic_slice_in_dim(pre_grad, offset, block_units, 1)
        weight_block = lax.dynamic_slice_in_dim(w_in, offset, block_units, 1)
        term = lax.dot_general(grad_block, weight_block, (((1,), (1,)), ((), ())), preferred_element_type=jnp.float32)
        rounded = lax.optimization_barrier(term.astype(jnp.bfloat16))
        return (running + rounded.astype(jnp.float32), None)
    summed, _ = lax.scan(add_block, jnp.zeros((TOKENS, D), jnp.float32), jnp.arange(N_HID, dtype=jnp.int32))
    mix_grad = norm_backward(z_mix, gain_mix, ffn_grad + summed)
    spectrum = jnp.fft.ifft2(mix_grad)
    grad_in = mix_grad + jnp.real(spectrum) * math.sqrt(TOKENS * D)
    return (grad_in, grad_w_in, grad_w_out)
```

```python
import functools
import math

import jax
import jax.numpy as jnp
from jax import lax
from jax.experimental import pallas as pl
from jax.experimental.pallas import tpu as pltpu
from jax.sharding import PartitionSpec as P

epsilon = 1e-05
SPANS = ("seq", "sub")
TEAM = ("seq", "sub", "hid")
LANES = 128


def norm_parts(values):
    values = values.astype(jnp.float32)
    row_mean = jnp.mean(values, axis=-1, keepdims=True)
    centred = values - row_mean
    inv_std = lax.rsqrt(jnp.mean(centred * centred, axis=-1, keepdims=True) + epsilon)
    return (centred * inv_std, inv_std)


def norm_backward(values, gain_vec, upstream):
    unit_rows, inv_std = norm_parts(values)
    scaled = upstream * gain_vec
    return inv_std * (
        scaled
        - jnp.mean(scaled, axis=-1, keepdims=True)
        - unit_rows * jnp.mean(scaled * unit_rows, axis=-1, keepdims=True)
    )


def gelu_tanh(values):
    return jax.nn.gelu(values, approximate=True)


def shift_pairs(size, step):
    return [(i, (i + step) % size) for i in range(size)]


def turn(products, period):
    angles = (2.0 * math.pi / period) * (products % period).astype(jnp.float32)
    return (jnp.cos(angles), jnp.sin(angles))


def feature_table(width, slots, team):
    half = width // 2
    device = lax.broadcasted_iota(jnp.int32, (team, 2 * slots, width), 0)
    place = lax.broadcasted_iota(jnp.int32, (team, 2 * slots, width), 1)
    feat = lax.broadcasted_iota(jnp.int32, (team, 2 * slots, width), 2)
    feat = lax.optimization_barrier(feat)
    is_sin = place >= slots
    slot = device * slots + place % slots
    top = is_sin & (slot == 0)
    freq = jnp.where(top, half, slot)
    lag = jnp.where(is_sin & ~top, width - width // 4, 0)
    angles = (2.0 * math.pi / width) * ((freq * feat + lag) % width).astype(jnp.float32)
    table = jnp.where(slot < half, jnp.cos(angles), 0.0)
    return table.astype(jnp.bfloat16).reshape(team * 2 * slots, width)


def position_table(count):
    fine = 32
    coarse = count // fine
    col = lax.optimization_barrier(jnp.arange(count, dtype=jnp.int32))
    cos_a, sin_a = turn(fine * jnp.arange(coarse, dtype=jnp.int32)[:, None] * col[None], count)
    cos_b, sin_b = turn(jnp.arange(fine, dtype=jnp.int32)[:, None] * col[None], count)
    cos_a, sin_a = cos_a[:, None], sin_a[:, None]
    cos_b, sin_b = cos_b[None], sin_b[None]
    both = jnp.stack([cos_a * cos_b - sin_a * sin_b, -sin_a * cos_b - cos_a * sin_b])
    return both.astype(jnp.bfloat16).reshape(2 * count, count)


def combine(terms):
    total = None
    for factor, value in terms:
        if abs(factor) < 1e-12:
            continue
        if abs(factor - 1.0) < 1e-12:
            total = value if total is None else total + value
        elif abs(factor + 1.0) < 1e-12:
            total = -value if total is None else total - value
        else:
            part = factor * value
            total = part if total is None else total + part
    return total


def span_transform(parts, freq, spans):
    angles = [2.0 * math.pi * (r * freq % spans) / spans for r in range(spans)]
    real = combine([(math.cos(a), p) for a, p in zip(angles, parts)])
    imag = combine([(math.sin(a), p) for a, p in zip(angles, parts)])
    return (real, imag)


def position_kernel(spans, hids, slots, x_ref, mark_ref, twist_ref, tab_ref, o_ref, v_ref):
    rows_in = x_ref.shape[2]
    count = rows_in * hids
    own_rows = spans * slots

    @pl.when(pl.program_id(0) == 0)
    def _():
        mark = jnp.broadcast_to(mark_ref[...], (slots, LANES)) > 0.5
        for hid in range(hids):
            for piece in range(rows_in // LANES):
                lanes = slice(piece * LANES, (piece + 1) * LANES)
                at = hid * rows_in + piece * LANES
                blocks = [x_ref[r * hids + hid, :, lanes].astype(jnp.float32) for r in range(spans)]
                cos_parts = [b[:slots] for b in blocks]
                sin_parts = [b[slots:] for b in blocks]
                cos_half, sin_half = [], []
                for freq in range(spans // 2 + 1):
                    cos_half.append(span_transform(cos_parts, freq, spans))
                    sin_half.append(span_transform(sin_parts, freq, spans))
                held = []
                for freq in range(spans):
                    low = min(freq, spans - freq)
                    c_re, c_im = cos_half[low]
                    s_re, s_im = sin_half[low]
                    if c_im is None:
                        c_im, s_im = jnp.zeros_like(c_re), jnp.zeros_like(s_re)
                    elif low != freq:
                        c_im, s_im = -c_im, -s_im
                    t_re = jnp.broadcast_to(twist_ref[0, freq : freq + 1, at : at + LANES], c_re.shape)
                    t_im = jnp.broadcast_to(twist_ref[1, freq : freq + 1, at : at + LANES], c_re.shape)
                    pairs = (
                        (jnp.where(mark, c_re, c_re - s_im), jnp.where(mark, c_im, c_im + s_re)),
                        (jnp.where(mark, s_re, c_re + s_im), jnp.where(mark, s_im, c_im - s_re)),
                    )
                    held.append(
                        [(re * t_re - im * t_im, re * t_im + im * t_re) for re, im in pairs]
                    )
                    if freq % 2 == 1:
                        row = (freq - 1) * slots
                        for side in range(2):
                            for part in range(2):
                                v_ref[
                                    side * own_rows + row : side * own_rows + row + 2 * slots,
                                    part * count + at : part * count + at + LANES,
                                ] = jnp.concatenate(
                                    [held[0][side][part], held[1][side][part]], axis=0
                                ).astype(v_ref.dtype)
                        held = []

    res = jnp.dot(v_ref[...], tab_ref[...], preferred_element_type=jnp.float32)
    res = res.astype(o_ref.dtype)
    for dest in range(o_ref.shape[0]):
        for side in range(2):
            o_ref[dest, side] = res[
                side * own_rows : (side + 1) * own_rows, dest * LANES : (dest + 1) * LANES
            ]


def position_transform(got, mark, twist, table, spans, hids, slots):
    count = table.shape[1]
    share = count // spans
    team = spans * hids
    rows = spans * slots
    if hids == 2 and share == LANES and slots % 8 == 0 and spans % 2 == 0:
        dests = 2
        out = pl.pallas_call(
            functools.partial(position_kernel, spans, hids, slots),
            grid=(spans // dests,),
            in_specs=[
                pl.BlockSpec(got.shape, lambda i: (0, 0, 0)),
                pl.BlockSpec(mark.shape, lambda i: (0, 0)),
                pl.BlockSpec(twist.shape, lambda i: (0, 0, 0)),
                pl.BlockSpec((2 * count, dests * LANES), lambda i: (0, i)),
            ],
            out_specs=pl.BlockSpec((dests, hids, rows, LANES), lambda i: (i, 0, 0, 0)),
            out_shape=jax.ShapeDtypeStruct((spans, hids, rows, LANES), jnp.bfloat16),
            scratch_shapes=[pltpu.VMEM((2 * rows, 2 * count), jnp.bfloat16)],
            compiler_params=pltpu.CompilerParams(vmem_limit_bytes=32 << 20),
            cost_estimate=pl.CostEstimate(
                flops=2 * 2 * rows * 2 * count * count, bytes_accessed=6 << 20, transcendentals=0
            ),
            name="position_transform",
        )(got, mark, twist, table)
        return out.reshape(team, rows, share)
    wide = got.astype(jnp.float32).reshape(spans, hids, 2, slots, count // hids)
    wide = wide.transpose(2, 0, 3, 1, 4).reshape(2, spans, slots, count)
    ids = jnp.arange(spans, dtype=jnp.int32)
    cos_s, sin_s = turn(ids[:, None] * ids[None], spans)
    exact = lax.Precision.HIGHEST
    re = jnp.einsum("kr,crsn->cksn", cos_s, wide, precision=exact)
    im = jnp.einsum("kr,crsn->cksn", sin_s, wide, precision=exact)
    special = mark > 0.5
    v_re = jnp.stack([jnp.where(special, re[0], re[0] - im[1]), jnp.where(special, re[1], re[0] + im[1])])
    v_im = jnp.stack([jnp.where(special, im[0], im[0] + re[1]), jnp.where(special, im[1], im[0] - re[1])])
    t_re, t_im = twist[0][:, None], twist[1][:, None]
    both = jnp.concatenate([v_re * t_re - v_im * t_im, v_re * t_im + v_im * t_re], axis=-1)
    res = jnp.dot(
        both.astype(jnp.bfloat16).reshape(2 * rows, 2 * count), table, preferred_element_type=jnp.float32
    ).astype(jnp.bfloat16)
    res = res.reshape(2, rows, spans, share).transpose(2, 0, 1, 3)
    res = jnp.repeat(res, hids // 2, axis=1)
    return res.reshape(team, rows, share)


def finish_kernel(spans, slots, back_ref, pick_ref, own_ref, o_ref, held_ref):
    team = back_ref.shape[0]
    groups = held_ref.shape[0]
    for freq in range(spans):
        rows = slice(freq * slots, (freq + 1) * slots)
        block = jnp.concatenate(
            [back_ref[s].astype(jnp.float32)[rows] for s in range(team)], axis=0
        ).astype(jnp.bfloat16)
        value = lax.dot_general(
            block, pick_ref[...], (((0,), (0,)), ((), ())), preferred_element_type=jnp.float32
        )
        for g in range(groups):
            held_ref[g, pl.ds(freq, LANES, stride=spans), :] = value[:, g * LANES : (g + 1) * LANES]
    for g in range(groups):
        lanes = slice(g * LANES, (g + 1) * LANES)
        o_ref[:, lanes] = own_ref[:, lanes] + held_ref[g]


def finish(back, pick, own, spans, slots):
    team, rows, share = back.shape
    if share == LANES and slots % 8 == 0 and own.shape[1] % LANES == 0:
        return pl.pallas_call(
            functools.partial(finish_kernel, spans, slots),
            out_shape=jax.ShapeDtypeStruct(own.shape, jnp.float32),
            scratch_shapes=[pltpu.VMEM((own.shape[1] // LANES, own.shape[0], LANES), jnp.float32)],
            compiler_params=pltpu.CompilerParams(vmem_limit_bytes=32 << 20),
            cost_estimate=pl.CostEstimate(
                flops=2 * own.shape[0] * pick.size, bytes_accessed=5 << 20, transcendentals=0
            ),
            name="finish",
        )(back, pick, own)
    value = jnp.einsum(
        "skjn,sjm->nkm",
        back.reshape(team, spans, slots, share),
        pick.reshape(team, slots, pick.shape[1]),
        preferred_element_type=jnp.float32,
    )
    return own + value.reshape(own.shape)


def local(z_mix, z_ffn, pre_act, grad_out, gain_mix, gain_ffn, w_in, w_out):
    tok_rows, width = z_mix.shape
    unit_count = pre_act.shape[1]
    hids = lax.axis_size("hid")
    hid_index = lax.axis_index("hid")
    spans = lax.axis_size(SPANS)
    team = spans * hids
    half = width // 2
    slots = -(-half // team)
    rows = tok_rows // hids
    col_count = width // hids
    seq_length = tok_rows * spans
    bf16 = jnp.bfloat16

    def row_part(values, index):
        return lax.dynamic_slice_in_dim(values, index * rows, rows, 0)

    feat_tab = feature_table(width, slots, team)
    pos_tab = position_table(tok_rows)
    t_cos, t_sin = turn(
        jnp.arange(spans, dtype=jnp.int32)[:, None] * jnp.arange(tok_rows, dtype=jnp.int32)[None], seq_length
    )
    twist = jnp.stack([t_cos, t_sin]) * (1.0 / math.sqrt(seq_length * width))
    team_index = lax.axis_index(TEAM)
    mark = ((team_index * slots + jnp.arange(slots, dtype=jnp.int32)) == 0).astype(jnp.float32)[:, None]
    own_ids = hid_index * col_count + jnp.arange(col_count, dtype=jnp.int32)
    own_slot = jnp.where(own_ids < half, own_ids, jnp.where(own_ids == half, 0, width - own_ids))
    pick = (jnp.arange(team * slots, dtype=jnp.int32)[:, None] == own_slot[None]).astype(bf16)

    normed = (norm_parts(z_mix)[0] * gain_mix).astype(bf16)
    ffn_grad = norm_backward(z_ffn, gain_ffn, grad_out.astype(jnp.float32))
    ffn_low = ffn_grad.astype(bf16)
    pre_wide = pre_act.astype(jnp.float32)
    activation = gelu_tanh(pre_wide).astype(bf16)
    _, pull_back = jax.vjp(gelu_tanh, pre_wide)
    contract_units = (((1,), (1,)), ((), ()))
    contract_rows = (((0,), (0,)), ((), ()))
    act_grad = jnp.dot(
        ffn_low, lax.all_gather(w_out, SPANS, axis=0, tiled=True), preferred_element_type=jnp.float32
    )
    pre_grad = pull_back(act_grad)[0].astype(bf16)
    partial_sum = lax.dot_general(
        pre_grad,
        lax.all_gather(w_in, SPANS, axis=0, tiled=True),
        contract_units,
        preferred_element_type=jnp.float32,
    ).astype(bf16)
    both_grads = lax.psum_scatter(
        jnp.concatenate(
            [
                lax.dot_general(normed, pre_grad, contract_rows, preferred_element_type=jnp.float32),
                lax.dot_general(ffn_low, activation, contract_rows, preferred_element_type=jnp.float32),
            ],
            axis=1,
        ).astype(bf16),
        SPANS,
        scatter_dimension=0,
        tiled=True,
    ).astype(jnp.float32)
    grad_w_in = both_grads[:, :unit_count]
    grad_w_out = both_grads[:, unit_count:]

    summed = row_part(partial_sum, hid_index).astype(jnp.float32)
    for step in range(1, hids):
        sent = row_part(partial_sum, (hid_index + step) % hids)
        summed += lax.ppermute(sent, "hid", shift_pairs(hids, step)).astype(jnp.float32)
    mix_grad = norm_backward(
        row_part(z_mix, hid_index), gain_mix, row_part(ffn_grad, hid_index) + summed
    )
    mix_low = mix_grad.astype(bf16)

    spectral = lax.dot_general(
        feat_tab, mix_low, contract_units, preferred_element_type=jnp.float32
    ).astype(bf16)
    got = lax.all_to_all(
        spectral.reshape(team, 2 * slots, rows), TEAM, split_axis=0, concat_axis=0, tiled=True
    )
    sent_back = position_transform(got, mark, twist, pos_tab, spans, hids, slots)
    back = lax.all_to_all(sent_back, TEAM, split_axis=0, concat_axis=0, tiled=True)

    def col_part(values, index):
        return lax.dynamic_slice_in_dim(values, index * col_count, col_count, 1)

    own = jnp.zeros((tok_rows, col_count), jnp.float32)
    own = lax.dynamic_update_slice_in_dim(own, col_part(mix_grad, hid_index), hid_index * rows, 0)
    for step in range(1, hids):
        sent = col_part(mix_low, (hid_index + step) % hids)
        came = lax.ppermute(sent, "hid", shift_pairs(hids, step)).astype(jnp.float32)
        own = lax.dynamic_update_slice_in_dim(own, came, (hid_index - step) % hids * rows, 0)
    grad_in = finish(back, pick, own, spans, slots)
    return (grad_in, grad_w_in, grad_w_out)


def solution(mesh):
    in_specs = (
        P(("groups", "seq", "sub"), None),
        P(("groups", "seq", "sub"), None),
        P(("groups", "seq", "sub"), "hid"),
        P(("groups", "seq", "sub"), None),
        P(),
        P(),
        P(("seq", "sub"), "hid"),
        P(("seq", "sub"), "hid"),
    )
    out_specs = (
        P(("groups", "seq", "sub"), "hid"),
        P(("groups", "seq", "sub"), "hid"),
        P(("groups", "seq", "sub"), "hid"),
    )
    return jax.shard_map(local, mesh=mesh, in_specs=in_specs, out_specs=out_specs, check_vma=False)
```

```python
import functools
import math

import jax
import jax.numpy as jnp
from jax import lax
from jax.experimental import pallas as pl
from jax.experimental.pallas import tpu as pltpu
from jax.sharding import PartitionSpec as P

epsilon = 1e-05
SPANS = ("seq", "sub")
TEAM = ("seq", "sub", "hid")
LANES = 128


def norm_parts(values):
    values = values.astype(jnp.float32)
    row_mean = jnp.mean(values, axis=-1, keepdims=True)
    centred = values - row_mean
    inv_std = lax.rsqrt(jnp.mean(centred * centred, axis=-1, keepdims=True) + epsilon)
    return (centred * inv_std, inv_std)


def norm_backward(values, gain_vec, upstream):
    unit_rows, inv_std = norm_parts(values)
    scaled = upstream * gain_vec
    return inv_std * (
        scaled
        - jnp.mean(scaled, axis=-1, keepdims=True)
        - unit_rows * jnp.mean(scaled * unit_rows, axis=-1, keepdims=True)
    )


def gelu_tanh(values):
    return jax.nn.gelu(values, approximate=True)


def shift_pairs(size, step):
    return [(i, (i + step) % size) for i in range(size)]


def turn(products, period):
    angles = (2.0 * math.pi / period) * (products % period).astype(jnp.float32)
    return (jnp.cos(angles), jnp.sin(angles))


def feature_table(feats, width, slots, team):
    half = width // 2
    cos_a, sin_a = turn(slots * jnp.arange(team, dtype=jnp.int32)[:, None] * feats[None], width)
    cos_b, sin_b = turn(jnp.arange(slots, dtype=jnp.int32)[:, None] * feats[None], width)
    slot = lax.broadcasted_iota(jnp.int32, (team, slots, 1), 0) * slots
    slot = slot + lax.broadcasted_iota(jnp.int32, (team, slots, 1), 1)
    cos_all = cos_a[:, None] * cos_b[None] - sin_a[:, None] * sin_b[None]
    sin_all = sin_a[:, None] * cos_b[None] + cos_a[:, None] * sin_b[None]
    top = (1 - 2 * (feats % 2)).astype(jnp.float32)[None, None]
    sin_all = jnp.where(slot == 0, top, sin_all)
    table = jnp.where(slot < half, jnp.stack([cos_all, sin_all], axis=1).transpose(1, 0, 2, 3), 0.0)
    return table.astype(jnp.bfloat16).transpose(1, 0, 2, 3).reshape(team * 2 * slots, width)


def position_table(count, seed):
    fine = 32
    coarse = count // fine
    col = jnp.arange(count, dtype=jnp.int32) + seed
    cos_a, sin_a = turn(fine * jnp.arange(coarse, dtype=jnp.int32)[:, None] * col[None], count)
    cos_b, sin_b = turn(jnp.arange(fine, dtype=jnp.int32)[:, None] * col[None], count)
    cos_a, sin_a = cos_a[:, None], sin_a[:, None]
    cos_b, sin_b = cos_b[None], sin_b[None]
    both = jnp.stack([cos_a * cos_b - sin_a * sin_b, -sin_a * cos_b - cos_a * sin_b])
    return both.astype(jnp.bfloat16).reshape(2 * count, count)


def combine(terms):
    total = None
    for factor, value in terms:
        if abs(factor) < 1e-12:
            continue
        if abs(factor - 1.0) < 1e-12:
            total = value if total is None else total + value
        elif abs(factor + 1.0) < 1e-12:
            total = -value if total is None else total - value
        else:
            part = factor * value
            total = part if total is None else total + part
    return total


def span_transform(parts, freq, spans):
    angles = [2.0 * math.pi * (r * freq % spans) / spans for r in range(spans)]
    real = combine([(math.cos(a), p) for a, p in zip(angles, parts)])
    imag = combine([(math.sin(a), p) for a, p in zip(angles, parts)])
    return (real, imag)


def position_kernel(spans, hids, slots, x_ref, mark_ref, twist_ref, tab_ref, o_ref, v_ref):
    rows_in = x_ref.shape[2]
    count = rows_in * hids
    own_rows = spans * slots

    @pl.when(pl.program_id(0) == 0)
    def _():
        mark = jnp.broadcast_to(mark_ref[...], (slots, LANES)) > 0.5
        for hid in range(hids):
            for piece in range(rows_in // LANES):
                lanes = slice(piece * LANES, (piece + 1) * LANES)
                at = hid * rows_in + piece * LANES
                blocks = [x_ref[r * hids + hid, :, lanes].astype(jnp.float32) for r in range(spans)]
                cos_parts = [b[:slots] for b in blocks]
                sin_parts = [b[slots:] for b in blocks]
                cos_half, sin_half = [], []
                for freq in range(spans // 2 + 1):
                    cos_half.append(span_transform(cos_parts, freq, spans))
                    sin_half.append(span_transform(sin_parts, freq, spans))
                held = []
                for freq in range(spans):
                    low = min(freq, spans - freq)
                    c_re, c_im = cos_half[low]
                    s_re, s_im = sin_half[low]
                    if c_im is None:
                        c_im, s_im = jnp.zeros_like(c_re), jnp.zeros_like(s_re)
                    elif low != freq:
                        c_im, s_im = -c_im, -s_im
                    t_re = jnp.broadcast_to(twist_ref[0, freq : freq + 1, at : at + LANES], c_re.shape)
                    t_im = jnp.broadcast_to(twist_ref[1, freq : freq + 1, at : at + LANES], c_re.shape)
                    pairs = (
                        (jnp.where(mark, c_re, c_re - s_im), jnp.where(mark, c_im, c_im + s_re)),
                        (jnp.where(mark, s_re, c_re + s_im), jnp.where(mark, s_im, c_im - s_re)),
                    )
                    held.append(
                        [(re * t_re - im * t_im, re * t_im + im * t_re) for re, im in pairs]
                    )
                    if freq % 2 == 1:
                        row = (freq - 1) * slots
                        for side in range(2):
                            for part in range(2):
                                v_ref[
                                    side * own_rows + row : side * own_rows + row + 2 * slots,
                                    part * count + at : part * count + at + LANES,
                                ] = jnp.concatenate(
                                    [held[0][side][part], held[1][side][part]], axis=0
                                ).astype(v_ref.dtype)
                        held = []

    res = jnp.dot(v_ref[...], tab_ref[...], preferred_element_type=jnp.float32)
    res = res.astype(o_ref.dtype)
    for dest in range(o_ref.shape[0]):
        for side in range(2):
            o_ref[dest, side] = res[
                side * own_rows : (side + 1) * own_rows, dest * LANES : (dest + 1) * LANES
            ]


def position_transform(got, mark, twist, table, spans, hids, slots):
    count = table.shape[1]
    share = count // spans
    team = spans * hids
    rows = spans * slots
    if hids == 2 and share == LANES and slots % 8 == 0 and spans % 2 == 0:
        dests = 2
        out = pl.pallas_call(
            functools.partial(position_kernel, spans, hids, slots),
            grid=(spans // dests,),
            in_specs=[
                pl.BlockSpec(got.shape, lambda i: (0, 0, 0)),
                pl.BlockSpec(mark.shape, lambda i: (0, 0)),
                pl.BlockSpec(twist.shape, lambda i: (0, 0, 0)),
                pl.BlockSpec((2 * count, dests * LANES), lambda i: (0, i)),
            ],
            out_specs=pl.BlockSpec((dests, hids, rows, LANES), lambda i: (i, 0, 0, 0)),
            out_shape=jax.ShapeDtypeStruct((spans, hids, rows, LANES), jnp.bfloat16),
            scratch_shapes=[pltpu.VMEM((2 * rows, 2 * count), jnp.bfloat16)],
            compiler_params=pltpu.CompilerParams(vmem_limit_bytes=48 << 20),
            cost_estimate=pl.CostEstimate(
                flops=2 * 2 * rows * 2 * count * count, bytes_accessed=6 << 20, transcendentals=0
            ),
            name="position_transform",
        )(got, mark, twist, table)
        return out.reshape(team, rows, share)
    wide = got.astype(jnp.float32).reshape(spans, hids, 2, slots, count // hids)
    wide = wide.transpose(2, 0, 3, 1, 4).reshape(2, spans, slots, count)
    ids = jnp.arange(spans, dtype=jnp.int32)
    cos_s, sin_s = turn(ids[:, None] * ids[None], spans)
    exact = lax.Precision.HIGHEST
    re = jnp.einsum("kr,crsn->cksn", cos_s, wide, precision=exact)
    im = jnp.einsum("kr,crsn->cksn", sin_s, wide, precision=exact)
    special = mark > 0.5
    v_re = jnp.stack([jnp.where(special, re[0], re[0] - im[1]), jnp.where(special, re[1], re[0] + im[1])])
    v_im = jnp.stack([jnp.where(special, im[0], im[0] + re[1]), jnp.where(special, im[1], im[0] - re[1])])
    t_re, t_im = twist[0][:, None], twist[1][:, None]
    both = jnp.concatenate([v_re * t_re - v_im * t_im, v_re * t_im + v_im * t_re], axis=-1)
    res = jnp.dot(
        both.astype(jnp.bfloat16).reshape(2 * rows, 2 * count), table, preferred_element_type=jnp.float32
    ).astype(jnp.bfloat16)
    res = res.reshape(2, rows, spans, share).transpose(2, 0, 1, 3)
    res = jnp.repeat(res, hids // 2, axis=1)
    return res.reshape(team, rows, share)


def finish_kernel(spans, slots, back_ref, pick_ref, own_ref, o_ref, held_ref):
    team = back_ref.shape[0]
    groups = held_ref.shape[0]
    for freq in range(spans):
        rows = slice(freq * slots, (freq + 1) * slots)
        block = jnp.concatenate(
            [back_ref[s].astype(jnp.float32)[rows] for s in range(team)], axis=0
        ).astype(jnp.bfloat16)
        value = lax.dot_general(
            block, pick_ref[...], (((0,), (0,)), ((), ())), preferred_element_type=jnp.float32
        )
        for g in range(groups):
            held_ref[g, pl.ds(freq, LANES, stride=spans), :] = value[:, g * LANES : (g + 1) * LANES]
    for g in range(groups):
        lanes = slice(g * LANES, (g + 1) * LANES)
        o_ref[:, lanes] = own_ref[:, lanes] + held_ref[g]


def finish(back, pick, own, spans, slots):
    team, rows, share = back.shape
    if share == LANES and slots % 8 == 0 and own.shape[1] % LANES == 0:
        return pl.pallas_call(
            functools.partial(finish_kernel, spans, slots),
            out_shape=jax.ShapeDtypeStruct(own.shape, jnp.float32),
            scratch_shapes=[pltpu.VMEM((own.shape[1] // LANES, own.shape[0], LANES), jnp.float32)],
            compiler_params=pltpu.CompilerParams(vmem_limit_bytes=48 << 20),
            cost_estimate=pl.CostEstimate(
                flops=2 * own.shape[0] * pick.size, bytes_accessed=5 << 20, transcendentals=0
            ),
            name="finish",
        )(back, pick, own)
    value = jnp.einsum(
        "skjn,sjm->nkm",
        back.reshape(team, spans, slots, share),
        pick.reshape(team, slots, pick.shape[1]),
        preferred_element_type=jnp.float32,
    )
    return own + value.reshape(own.shape)


def weight_pieces(w_out, w_in):
    chips, cores, groups = (lax.axis_size(name) for name in ("seq", "sub", "groups"))
    mine = [w_out, w_in]
    if groups == 2:
        mine = [jnp.where(lax.axis_index("groups") == 0, w_out, w_in)]
    near = [((0, 0), (w_out, w_in))]
    steps = sorted(range(1, chips), key=lambda d: (min(d, chips - d), d))
    waves = [steps[k : k + 2] for k in range(0, len(steps), 2)]
    arrived = []
    for wave in waves:
        if arrived:
            mine = lax.optimization_barrier((tuple(mine), arrived[-1]))[0]
        came = []
        for d in wave:
            blocks = tuple(lax.ppermute(w, "seq", shift_pairs(chips, d)) for w in mine)
            came.extend(blocks)
            near.append(((d, 0), blocks))
            if groups == 2:
                near.append(((d, 1), (lax.ppermute(blocks[0], "groups", shift_pairs(2, 1)),)))
        arrived.append(came)
    pieces = [((0, d, k), arrays) for (d, k), arrays in near]
    for e in range(1, cores):
        for (d, k), arrays in near:
            pieces.append(
                ((e, d, k), tuple(lax.ppermute(x, "sub", shift_pairs(cores, -e)) for x in arrays))
            )
    return pieces, arrived


def piece_rows(key, width, shard, seq, sub, group, chips, cores):
    e, d, k = key
    row = (lax.rem(seq + chips - d, chips) * cores + lax.rem(sub + e, cores)) * shard
    if d and lax.axis_size("groups") == 2:
        return [row + lax.rem(group + k, 2) * width]
    return [row, row + width]


def feed_kernel(keys, count, shard, chips, cores, carried, where_ref, x_ref, slope_ref, *refs):
    blocks, refs = list(refs[:count]), refs[count + carried :]
    pre_ref, part_ref, weights, total = refs
    width = x_ref.shape[1]
    for key in keys:
        for at in piece_rows(key, width, shard, where_ref[1], where_ref[2], where_ref[3], chips, cores):
            weights[pl.ds(pl.multiple_of(at, shard), shard), :] = blocks.pop(0)[...]
    act_grad = jnp.dot(x_ref[...], weights[:width, :], preferred_element_type=jnp.float32)
    pre_grad = (slope_ref[...] * act_grad).astype(jnp.bfloat16)
    pre_ref[...] = pre_grad
    term = lax.dot_general(
        pre_grad, weights[width:, :], (((1,), (1,)), ((), ())), preferred_element_type=jnp.float32
    )
    first = pl.program_id(0) == 0

    @pl.when(first)
    def _():
        total[...] = term

    @pl.when(jnp.logical_not(first))
    def _():
        total[...] += term

    @pl.when(pl.program_id(0) == pl.num_programs(0) - 1)
    def _():
        part_ref[...] = total[...].astype(part_ref.dtype)


def feed_rows(where, low, slope, pieces, rows, step, carried):
    chips, cores, hids = (lax.axis_size(name) for name in ("seq", "sub", "hid"))
    width, units = low.shape[1], slope.shape[1]
    shard = pieces[0][1][0].shape[0]
    tile = 768 if units % 768 == 0 else 128
    keys = [key for key, _ in pieces]
    flat = [x for _, arrays in pieces for x in arrays]

    def row_block(i, where_ref):
        return (lax.rem(where_ref[0] + step, hids), i)

    extra = [] if carried is None else [carried]
    return pl.pallas_call(
        functools.partial(feed_kernel, keys, len(flat), shard, chips, cores, len(extra)),
        grid_spec=pltpu.PrefetchScalarGridSpec(
            num_scalar_prefetch=1,
            grid=(units // tile,),
            in_specs=[
                pl.BlockSpec((rows, width), lambda i, w: (lax.rem(w[0] + step, hids), 0)),
                pl.BlockSpec((rows, tile), row_block),
                *[pl.BlockSpec((x.shape[0], tile), lambda i, w: (0, i)) for x in flat],
                *[pl.BlockSpec(memory_space=pl.ANY) for _ in extra],
            ],
            out_specs=[
                pl.BlockSpec((rows, tile), row_block),
                pl.BlockSpec((rows, width), lambda i, w: (0, 0)),
            ],
            scratch_shapes=[
                pltpu.VMEM((2 * width, tile), jnp.bfloat16),
                pltpu.VMEM((rows, width), jnp.float32),
            ],
        ),
        out_shape=[
            jax.ShapeDtypeStruct(slope.shape, jnp.bfloat16),
            jax.ShapeDtypeStruct((rows, width), jnp.bfloat16),
        ],
        input_output_aliases={3 + len(flat): 0} if extra else {},
        compiler_params=pltpu.CompilerParams(vmem_limit_bytes=48 << 20),
        cost_estimate=pl.CostEstimate(
            flops=4 * rows * width * units, bytes_accessed=12 << 20, transcendentals=0
        ),
        name="feed_rows",
    )(where, low, slope, *flat, *extra)


def whole_weights(pieces, width):
    chips, cores = lax.axis_size("seq"), lax.axis_size("sub")
    shard, units = pieces[0][1][0].shape
    places = [lax.axis_index(name) for name in ("seq", "sub", "groups")]
    whole = jnp.zeros((2 * width, units), jnp.bfloat16)
    for key, arrays in pieces:
        for at, x in zip(piece_rows(key, width, shard, *places, chips, cores), arrays):
            whole = lax.dynamic_update_slice_in_dim(whole, x, at, 0)
    return whole


def local(z_mix, z_ffn, pre_act, grad_out, gain_mix, gain_ffn, w_in, w_out):
    tok_rows, width = z_mix.shape
    unit_count = pre_act.shape[1]
    hids = lax.axis_size("hid")
    hid_index = lax.axis_index("hid")
    cores = lax.axis_size("sub")
    chips = lax.axis_size("seq")
    spans = chips * cores
    team = spans * hids
    half = width // 2
    slots = -(-half // team)
    rows = tok_rows // hids
    col_count = width // hids
    seq_length = tok_rows * spans
    shard_rows = w_in.shape[0]
    bf16 = jnp.bfloat16
    contract_units = (((1,), (1,)), ((), ()))
    contract_rows = (((0,), (0,)), ((), ()))

    def row_part(values, index):
        return lax.dynamic_slice_in_dim(values, index * rows, rows, 0)

    pieces, arrived = weight_pieces(w_out, w_in)
    where = jnp.stack([lax.axis_index(name) for name in ("hid", "seq", "sub", "groups")])

    feats = jnp.arange(width, dtype=jnp.int32)
    core_ids = (lax.axis_index("sub") + jnp.arange(cores, dtype=jnp.int32)) % cores
    core_order = (
        jnp.arange(chips, dtype=jnp.int32)[None, :, None] * cores + core_ids[:, None, None]
    ) * shard_rows + jnp.arange(shard_rows, dtype=jnp.int32)[None, None]
    core_reorder = (feats[:, None] == core_order.reshape(1, width)).astype(bf16)

    def by_core(values):
        return jnp.dot(values, core_reorder, preferred_element_type=jnp.float32).astype(bf16)

    ffn_grad = norm_backward(z_ffn, gain_ffn, grad_out.astype(jnp.float32))
    ffn_low = ffn_grad.astype(bf16)
    ffn_core = by_core(ffn_low)
    ffn_low, ffn_core, pre_act, *_ = lax.optimization_barrier((ffn_low, ffn_core, pre_act, *arrived[0]))
    pre_wide = pre_act.astype(jnp.float32)
    activation, pull_back = jax.vjp(gelu_tanh, pre_wide)
    activation = activation.astype(bf16)
    slope = pull_back(jnp.ones_like(pre_wide))[0]
    activation, slope = lax.optimization_barrier((activation, slope))

    def weight_grad(left, right, after):
        def core_rows(core):
            part = left[:, core * (width // cores) : (core + 1) * (width // cores)]
            return lax.dot_general(part, right, contract_rows, preferred_element_type=jnp.float32)

        total = core_rows(0)
        for core in range(1, cores):
            sent = core_rows(core).astype(bf16)
            total += lax.ppermute(sent, "sub", shift_pairs(cores, core)).astype(jnp.float32)
        total, *_ = lax.optimization_barrier((total.astype(bf16), *after))
        return lax.psum_scatter(total, "seq", scatter_dimension=0, tiled=True).astype(jnp.float32)

    grad_w_out = weight_grad(ffn_core, activation, arrived[-1])

    partials = []
    if shard_rows % 16 == 0 and rows % 16 == 0 and unit_count % 128 == 0:
        pre_grad = None
        for step in [*range(1, hids), 0]:
            pre_grad, part = feed_rows(where, ffn_low, slope, pieces, rows, step, pre_grad)
            partials.append(part)
    else:
        whole = whole_weights(pieces, width)
        act_grad = jnp.dot(ffn_low, whole[:width], preferred_element_type=jnp.float32)
        pre_grad = (slope * act_grad).astype(bf16)
        product = lax.dot_general(
            pre_grad, whole[width:], contract_units, preferred_element_type=jnp.float32
        ).astype(bf16)
        for step in [*range(1, hids), 0]:
            partials.append(row_part(product, (hid_index + step) % hids))

    seed = jnp.zeros((), jnp.int32)
    late_z, seed, *_ = lax.optimization_barrier((z_mix, seed, *partials[:-1]))
    normed_core = by_core((norm_parts(late_z)[0] * gain_mix).astype(bf16))
    feat_tab = lax.optimization_barrier(feature_table(feats + seed, width, slots, team))
    pos_tab = lax.optimization_barrier(position_table(tok_rows, seed))
    t_cos, t_sin = turn(
        jnp.arange(spans, dtype=jnp.int32)[:, None] * jnp.arange(tok_rows, dtype=jnp.int32)[None], seq_length
    )
    twist = jnp.stack([t_cos, t_sin]) * (1.0 / math.sqrt(seq_length * width))
    team_index = lax.axis_index(TEAM)
    mark = ((team_index * slots + jnp.arange(slots, dtype=jnp.int32)) == 0).astype(jnp.float32)[:, None]
    own_ids = hid_index * col_count + jnp.arange(col_count, dtype=jnp.int32)
    own_slot = jnp.where(own_ids < half, own_ids, jnp.where(own_ids == half, 0, width - own_ids))
    pick = (jnp.arange(team * slots, dtype=jnp.int32)[:, None] == own_slot[None]).astype(bf16)

    summed = partials.pop().astype(jnp.float32)
    for step, sent in enumerate(partials, 1):
        summed += lax.ppermute(sent, "hid", shift_pairs(hids, step)).astype(jnp.float32)
    mix_grad = norm_backward(
        row_part(z_mix, hid_index), gain_mix, row_part(ffn_grad, hid_index) + summed
    )
    mix_low = mix_grad.astype(bf16)

    spectral = lax.dot_general(
        feat_tab, mix_low, contract_units, preferred_element_type=jnp.float32
    ).astype(bf16)
    pre_grad, *_ = lax.optimization_barrier((pre_grad, spectral))
    grad_w_in = weight_grad(normed_core, pre_grad, ())
    got = lax.all_to_all(
        spectral.reshape(team, 2 * slots, rows), TEAM, split_axis=0, concat_axis=0, tiled=True
    )
    def col_part(values, index):
        return lax.dynamic_slice_in_dim(values, index * col_count, col_count, 1)

    own = jnp.zeros((tok_rows, col_count), jnp.float32)
    own = lax.dynamic_update_slice_in_dim(own, col_part(mix_grad, hid_index), hid_index * rows, 0)
    for step in range(1, hids):
        sent = col_part(mix_low, (hid_index + step) % hids)
        came = lax.ppermute(sent, "hid", shift_pairs(hids, step)).astype(jnp.float32)
        own = lax.dynamic_update_slice_in_dim(own, came, (hid_index - step) % hids * rows, 0)
    got, own = lax.optimization_barrier((got, own))
    sent_back = position_transform(got, mark, twist, pos_tab, spans, hids, slots)
    back = lax.all_to_all(sent_back, TEAM, split_axis=0, concat_axis=0, tiled=True)
    back, grad_w_in, grad_w_out = lax.optimization_barrier((back, grad_w_in, grad_w_out))
    grad_in = finish(back, pick, own, spans, slots)
    return (grad_in, grad_w_in, grad_w_out)


def solution(mesh):
    in_specs = (
        P(("groups", "seq", "sub"), None),
        P(("groups", "seq", "sub"), None),
        P(("groups", "seq", "sub"), "hid"),
        P(("groups", "seq", "sub"), None),
        P(),
        P(),
        P(("seq", "sub"), "hid"),
        P(("seq", "sub"), "hid"),
    )
    out_specs = (
        P(("groups", "seq", "sub"), "hid"),
        P(("groups", "seq", "sub"), "hid"),
        P(("groups", "seq", "sub"), "hid"),
    )
    return jax.shard_map(local, mesh=mesh, in_specs=in_specs, out_specs=out_specs, check_vma=False)
```

```python
import functools
import math

import jax
import jax.numpy as jnp
from jax import lax
from jax.experimental import pallas as pl
from jax.experimental.pallas import tpu as pltpu
from jax.sharding import PartitionSpec as P

epsilon = 1e-05
SPANS = ("seq", "sub")
TEAM = ("seq", "sub", "hid")
LANES = 128
ROWS = 128
SMALL = pl.CostEstimate(flops=1 << 20, bytes_accessed=1 << 16, transcendentals=0)


def norm_parts(values):
    values = values.astype(jnp.float32)
    row_mean = jnp.mean(values, axis=-1, keepdims=True)
    centred = values - row_mean
    inv_std = lax.rsqrt(jnp.mean(centred * centred, axis=-1, keepdims=True) + epsilon)
    return (centred * inv_std, inv_std)


def norm_backward(values, gain_vec, upstream):
    unit_rows, inv_std = norm_parts(values)
    scaled = upstream * gain_vec
    return inv_std * (
        scaled
        - jnp.mean(scaled, axis=-1, keepdims=True)
        - unit_rows * jnp.mean(scaled * unit_rows, axis=-1, keepdims=True)
    )


def gelu_tanh(values):
    return jax.nn.gelu(values, approximate=True)


def shift_pairs(size, step):
    return [(i, (i + step) % size) for i in range(size)]


def turn(products, period):
    angles = (2.0 * math.pi / period) * (products % period).astype(jnp.float32)
    return (jnp.cos(angles), jnp.sin(angles))


def feature_table(feats, seed, width, slots, team):
    half = width // 2
    cos_a, sin_a = turn(slots * (jnp.arange(team, dtype=jnp.int32) + seed)[:, None] * feats[None], width)
    cos_b, sin_b = turn((jnp.arange(slots, dtype=jnp.int32) + seed)[:, None] * feats[None], width)
    slot = lax.broadcasted_iota(jnp.int32, (team, slots, 1), 0) * slots
    slot = slot + lax.broadcasted_iota(jnp.int32, (team, slots, 1), 1)
    cos_all = cos_a[:, None] * cos_b[None] - sin_a[:, None] * sin_b[None]
    sin_all = sin_a[:, None] * cos_b[None] + cos_a[:, None] * sin_b[None]
    top = (1 - 2 * (feats % 2)).astype(jnp.float32)[None, None]
    sin_all = jnp.where(slot == 0, top, sin_all)
    table = jnp.where(slot < half, jnp.stack([cos_all, sin_all], axis=1).transpose(1, 0, 2, 3), 0.0)
    return table.astype(jnp.bfloat16).transpose(1, 0, 2, 3).reshape(team * 2 * slots, width)


def position_table(count, seed):
    fine = 32
    coarse = count // fine
    col = jnp.arange(count, dtype=jnp.int32) + seed
    cos_a, sin_a = turn(fine * (jnp.arange(coarse, dtype=jnp.int32) + seed)[:, None] * col[None], count)
    cos_b, sin_b = turn((jnp.arange(fine, dtype=jnp.int32) + seed)[:, None] * col[None], count)
    cos_a, sin_a = cos_a[:, None], sin_a[:, None]
    cos_b, sin_b = cos_b[None], sin_b[None]
    both = jnp.stack([cos_a * cos_b - sin_a * sin_b, -sin_a * cos_b - cos_a * sin_b])
    return both.astype(jnp.bfloat16).reshape(2 * count, count)


def combine(terms):
    total = None
    for factor, value in terms:
        if abs(factor) < 1e-12:
            continue
        if abs(factor - 1.0) < 1e-12:
            total = value if total is None else total + value
        elif abs(factor + 1.0) < 1e-12:
            total = -value if total is None else total - value
        else:
            part = factor * value
            total = part if total is None else total + part
    return total


def span_transform(parts, freq, spans):
    angles = [2.0 * math.pi * (r * freq % spans) / spans for r in range(spans)]
    real = combine([(math.cos(a), p) for a, p in zip(angles, parts)])
    imag = combine([(math.sin(a), p) for a, p in zip(angles, parts)])
    return (real, imag)


def position_kernel(spans, hids, slots, x_ref, mark_ref, twist_ref, tab_ref, o_ref, v_ref):
    rows_in = x_ref.shape[2]
    count = rows_in * hids
    own_rows = spans * slots

    @pl.when(pl.program_id(0) == 0)
    def _():
        mark = jnp.broadcast_to(mark_ref[...], (slots, LANES)) > 0.5
        for hid in range(hids):
            for piece in range(rows_in // LANES):
                lanes = slice(piece * LANES, (piece + 1) * LANES)
                at = hid * rows_in + piece * LANES
                blocks = [x_ref[r * hids + hid, :, lanes].astype(jnp.float32) for r in range(spans)]
                cos_parts = [b[:slots] for b in blocks]
                sin_parts = [b[slots:] for b in blocks]
                cos_half, sin_half = [], []
                for freq in range(spans // 2 + 1):
                    cos_half.append(span_transform(cos_parts, freq, spans))
                    sin_half.append(span_transform(sin_parts, freq, spans))
                held = []
                for freq in range(spans):
                    low = min(freq, spans - freq)
                    c_re, c_im = cos_half[low]
                    s_re, s_im = sin_half[low]
                    if c_im is None:
                        c_im, s_im = jnp.zeros_like(c_re), jnp.zeros_like(s_re)
                    elif low != freq:
                        c_im, s_im = -c_im, -s_im
                    t_re = jnp.broadcast_to(twist_ref[0, freq : freq + 1, at : at + LANES], c_re.shape)
                    t_im = jnp.broadcast_to(twist_ref[1, freq : freq + 1, at : at + LANES], c_re.shape)
                    pairs = (
                        (jnp.where(mark, c_re, c_re - s_im), jnp.where(mark, c_im, c_im + s_re)),
                        (jnp.where(mark, s_re, c_re + s_im), jnp.where(mark, s_im, c_im - s_re)),
                    )
                    held.append(
                        [(re * t_re - im * t_im, re * t_im + im * t_re) for re, im in pairs]
                    )
                    if freq % 2 == 1:
                        row = (freq - 1) * slots
                        for side in range(2):
                            for part in range(2):
                                v_ref[
                                    side * own_rows + row : side * own_rows + row + 2 * slots,
                                    part * count + at : part * count + at + LANES,
                                ] = jnp.concatenate(
                                    [held[0][side][part], held[1][side][part]], axis=0
                                ).astype(v_ref.dtype)
                        held = []

    res = jnp.dot(v_ref[...], tab_ref[...], preferred_element_type=jnp.float32)
    res = res.astype(o_ref.dtype)
    for dest in range(o_ref.shape[0]):
        for side in range(2):
            o_ref[dest, side] = res[
                side * own_rows : (side + 1) * own_rows, dest * LANES : (dest + 1) * LANES
            ]


def position_transform(got, mark, twist, table, spans, hids, slots):
    count = table.shape[1]
    share = count // spans
    team = spans * hids
    rows = spans * slots
    if hids == 2 and share == LANES and slots % 8 == 0 and spans % 2 == 0:
        dests = 2
        out = pl.pallas_call(
            functools.partial(position_kernel, spans, hids, slots),
            grid=(spans // dests,),
            in_specs=[
                pl.BlockSpec(got.shape, lambda i: (0, 0, 0)),
                pl.BlockSpec(mark.shape, lambda i: (0, 0)),
                pl.BlockSpec(twist.shape, lambda i: (0, 0, 0)),
                pl.BlockSpec((2 * count, dests * LANES), lambda i: (0, i)),
            ],
            out_specs=pl.BlockSpec((dests, hids, rows, LANES), lambda i: (i, 0, 0, 0)),
            out_shape=jax.ShapeDtypeStruct((spans, hids, rows, LANES), jnp.bfloat16),
            scratch_shapes=[pltpu.VMEM((2 * rows, 2 * count), jnp.bfloat16)],
            compiler_params=pltpu.CompilerParams(vmem_limit_bytes=58 << 20),
            cost_estimate=pl.CostEstimate(
                flops=2 * 2 * rows * 2 * count * count, bytes_accessed=6 << 20, transcendentals=0
            ),
            name="position_transform",
        )(got, mark, twist, table)
        return out.reshape(team, rows, share)
    wide = got.astype(jnp.float32).reshape(spans, hids, 2, slots, count // hids)
    wide = wide.transpose(2, 0, 3, 1, 4).reshape(2, spans, slots, count)
    ids = jnp.arange(spans, dtype=jnp.int32)
    cos_s, sin_s = turn(ids[:, None] * ids[None], spans)
    exact = lax.Precision.HIGHEST
    re = jnp.einsum("kr,crsn->cksn", cos_s, wide, precision=exact)
    im = jnp.einsum("kr,crsn->cksn", sin_s, wide, precision=exact)
    special = mark > 0.5
    v_re = jnp.stack([jnp.where(special, re[0], re[0] - im[1]), jnp.where(special, re[1], re[0] + im[1])])
    v_im = jnp.stack([jnp.where(special, im[0], im[0] + re[1]), jnp.where(special, im[1], im[0] - re[1])])
    t_re, t_im = twist[0][:, None], twist[1][:, None]
    both = jnp.concatenate([v_re * t_re - v_im * t_im, v_re * t_im + v_im * t_re], axis=-1)
    res = jnp.dot(
        both.astype(jnp.bfloat16).reshape(2 * rows, 2 * count), table, preferred_element_type=jnp.float32
    ).astype(jnp.bfloat16)
    res = res.reshape(2, rows, spans, share).transpose(2, 0, 1, 3)
    res = jnp.repeat(res, hids // 2, axis=1)
    return res.reshape(team, rows, share)


def finish_kernel(spans, slots, back_ref, pick_ref, own_ref, o_ref, held_ref):
    team = back_ref.shape[0]
    groups = held_ref.shape[0]
    for freq in range(spans):
        rows = slice(freq * slots, (freq + 1) * slots)
        block = jnp.concatenate(
            [back_ref[s].astype(jnp.float32)[rows] for s in range(team)], axis=0
        ).astype(jnp.bfloat16)
        value = lax.dot_general(
            block, pick_ref[...], (((0,), (0,)), ((), ())), preferred_element_type=jnp.float32
        )
        for g in range(groups):
            held_ref[g, pl.ds(freq, LANES, stride=spans), :] = value[:, g * LANES : (g + 1) * LANES]
    for g in range(groups):
        lanes = slice(g * LANES, (g + 1) * LANES)
        o_ref[:, lanes] = own_ref[:, lanes] + held_ref[g]


def finish(back, pick, own, spans, slots):
    team, rows, share = back.shape
    if share == LANES and slots % 8 == 0 and own.shape[1] % LANES == 0:
        return pl.pallas_call(
            functools.partial(finish_kernel, spans, slots),
            out_shape=jax.ShapeDtypeStruct(own.shape, jnp.float32),
            scratch_shapes=[pltpu.VMEM((own.shape[1] // LANES, own.shape[0], LANES), jnp.float32)],
            compiler_params=pltpu.CompilerParams(vmem_limit_bytes=48 << 20),
            cost_estimate=pl.CostEstimate(
                flops=2 * own.shape[0] * pick.size, bytes_accessed=5 << 20, transcendentals=0
            ),
            name="finish",
        )(back, pick, own)
    value = jnp.einsum(
        "skjn,sjm->nkm",
        back.reshape(team, spans, slots, share),
        pick.reshape(team, slots, pick.shape[1]),
        preferred_element_type=jnp.float32,
    )
    return own + value.reshape(own.shape)


def ffn_norm_kernel(z_ref, up_ref, gain_ref, grad_ref, low_ref):
    grad = norm_backward(z_ref[...], gain_ref[...], up_ref[...].astype(jnp.float32))
    low = grad.astype(jnp.bfloat16)
    grad_ref[...] = grad
    low_ref[...] = low


def ffn_norm(z_ffn, grad_out, gain):
    rows, width = z_ffn.shape
    tile = pl.BlockSpec((ROWS, width), lambda i: (i, 0))
    return pl.pallas_call(
        ffn_norm_kernel,
        grid=(rows // ROWS,),
        in_specs=[tile, tile, pl.BlockSpec((1, width), lambda i: (0, 0))],
        out_specs=[tile, tile],
        out_shape=[
            jax.ShapeDtypeStruct(z_ffn.shape, jnp.float32),
            jax.ShapeDtypeStruct(z_ffn.shape, jnp.bfloat16),
        ],
        compiler_params=pltpu.CompilerParams(vmem_limit_bytes=32 << 20),
        cost_estimate=SMALL,
        name="ffn_norm",
    )(z_ffn, grad_out, gain[None])


def mix_norm_kernel(z_ref, gain_ref, order_ref, core_ref):
    normed = (norm_parts(z_ref[...])[0] * gain_ref[...]).astype(jnp.bfloat16)
    core_ref[...] = jnp.dot(normed, order_ref[...], preferred_element_type=jnp.float32).astype(jnp.bfloat16)


def mix_norm(z_mix, gain, order):
    rows, width = z_mix.shape
    tile = pl.BlockSpec((ROWS, width), lambda i: (i, 0))
    return pl.pallas_call(
        mix_norm_kernel,
        grid=(rows // ROWS,),
        in_specs=[tile, pl.BlockSpec((1, width), lambda i: (0, 0)), pl.BlockSpec(order.shape, lambda i: (0, 0))],
        out_specs=tile,
        out_shape=jax.ShapeDtypeStruct(z_mix.shape, jnp.bfloat16),
        compiler_params=pltpu.CompilerParams(vmem_limit_bytes=32 << 20),
        cost_estimate=SMALL,
        name="mix_norm",
    )(z_mix, gain[None], order)


def gelu_slope(values):
    scale = math.sqrt(2.0 / math.pi)
    a = values.astype(jnp.float32)
    square = a * a
    tanh = jnp.tanh(scale * a * (1.0 + 0.044715 * square))
    upper = 0.5 * (1.0 + tanh)
    return upper + (0.5 * scale) * a * (1.0 - tanh * tanh) * (1.0 + (3.0 * 0.044715) * square)


def mix_kernel(count, hids, where_ref, z_ref, ffn_ref, gain_ref, tab_ref, *refs):
    parts, (mix_ref, spec_ref) = refs[:count], refs[count:]
    summed = parts[0][...].astype(jnp.float32)
    for part in parts[1:]:
        summed += part[...].astype(jnp.float32)
    mix = norm_backward(z_ref[...], gain_ref[...], ffn_ref[...] + summed)
    low = mix.astype(jnp.bfloat16)
    mix_ref[...] = low
    spec_ref[...] = lax.dot_general(
        tab_ref[...], low, (((1,), (1,)), ((), ())), preferred_element_type=jnp.float32
    ).astype(jnp.bfloat16)


def mix_rows(where, z_mix, ffn_grad, gain, table, parts, hids):
    rows, width = parts[0].shape
    steps = rows // ROWS
    tile = pl.BlockSpec((ROWS, width), lambda i, w: (i, 0))
    own = pl.BlockSpec((ROWS, width), lambda i, w: (w[0] * steps + i, 0))
    return pl.pallas_call(
        functools.partial(mix_kernel, len(parts), hids),
        grid_spec=pltpu.PrefetchScalarGridSpec(
            num_scalar_prefetch=1,
            grid=(steps,),
            in_specs=[
                own,
                own,
                pl.BlockSpec((1, width), lambda i, w: (0, 0)),
                pl.BlockSpec(table.shape, lambda i, w: (0, 0)),
                *[tile for _ in parts],
            ],
            out_specs=[tile, pl.BlockSpec((table.shape[0], ROWS), lambda i, w: (0, i))],
        ),
        out_shape=[
            jax.ShapeDtypeStruct((rows, width), jnp.bfloat16),
            jax.ShapeDtypeStruct((table.shape[0], rows), jnp.bfloat16),
        ],
        compiler_params=pltpu.CompilerParams(vmem_limit_bytes=32 << 20),
        cost_estimate=SMALL,
        name="mix_rows",
    )(where, z_mix, ffn_grad, gain[None], table, *parts)


def weight_pieces(w_out, w_in, first):
    chips, cores, groups = (lax.axis_size(name) for name in ("seq", "sub", "groups"))
    mine = [w_out, w_in]
    if groups == 2:
        mine = [jnp.where(lax.axis_index("groups") == 0, w_out, w_in)]
    near = [((0, 0), (w_out, w_in))]
    steps = sorted(range(1, chips), key=lambda d: (min(d, chips - d), d))
    waves = [steps[k : k + 2] for k in range(0, len(steps), 2)]
    arrived = []
    for wave in waves:
        if arrived:
            mine = lax.optimization_barrier((tuple(mine), arrived[-1], first))[0]
        came = []
        for d in wave:
            blocks = tuple(lax.ppermute(w, "seq", shift_pairs(chips, d)) for w in mine)
            came.extend(blocks)
            near.append(((d, 0), blocks))
            if groups == 2:
                near.append(((d, 1), (lax.ppermute(blocks[0], "groups", shift_pairs(2, 1)),)))
        arrived.append(came)
    pieces = [((0, d, k), arrays) for (d, k), arrays in near]
    for e in range(1, cores):
        for (d, k), arrays in near:
            pieces.append(
                ((e, d, k), tuple(lax.ppermute(x, "sub", shift_pairs(cores, -e)) for x in arrays))
            )
    return pieces, arrived


def piece_rows(key, width, shard, seq, sub, group, chips, cores):
    e, d, k = key
    row = (lax.rem(seq + chips - d, chips) * cores + lax.rem(sub + e, cores)) * shard
    if d and lax.axis_size("groups") == 2:
        return [row + lax.rem(group + k, 2) * width]
    return [row, row + width]


def feed_kernel(keys, count, shard, chips, cores, carried, where_ref, x_ref, pre_act_ref, *refs):
    blocks, refs = list(refs[:count]), refs[count + carried :]
    pre_ref, part_ref, weights, total = refs
    width = x_ref.shape[1]
    for key in keys:
        for at in piece_rows(key, width, shard, where_ref[1], where_ref[2], where_ref[3], chips, cores):
            weights[pl.ds(pl.multiple_of(at, shard), shard), :] = blocks.pop(0)[...]
    act_grad = jnp.dot(x_ref[...], weights[:width, :], preferred_element_type=jnp.float32)
    pre_grad = (gelu_slope(pre_act_ref[...]) * act_grad).astype(jnp.bfloat16)
    pre_ref[...] = pre_grad
    term = lax.dot_general(
        pre_grad, weights[width:, :], (((1,), (1,)), ((), ())), preferred_element_type=jnp.float32
    )
    first = pl.program_id(0) == 0

    @pl.when(first)
    def _():
        total[...] = term

    @pl.when(jnp.logical_not(first))
    def _():
        total[...] += term

    @pl.when(pl.program_id(0) == pl.num_programs(0) - 1)
    def _():
        part_ref[...] = total[...].astype(part_ref.dtype)


def feed_rows(where, low, pre_act, pieces, rows, step, carried):
    chips, cores, hids = (lax.axis_size(name) for name in ("seq", "sub", "hid"))
    width, units = low.shape[1], pre_act.shape[1]
    shard = pieces[0][1][0].shape[0]
    tile = 768 if units % 768 == 0 else 128
    keys = [key for key, _ in pieces]
    flat = [x for _, arrays in pieces for x in arrays]

    def row_block(i, where_ref):
        return (lax.rem(where_ref[0] + step, hids), i)

    extra = [] if carried is None else [carried]
    return pl.pallas_call(
        functools.partial(feed_kernel, keys, len(flat), shard, chips, cores, len(extra)),
        grid_spec=pltpu.PrefetchScalarGridSpec(
            num_scalar_prefetch=1,
            grid=(units // tile,),
            in_specs=[
                pl.BlockSpec((rows, width), lambda i, w: (lax.rem(w[0] + step, hids), 0)),
                pl.BlockSpec((rows, tile), row_block),
                *[pl.BlockSpec((x.shape[0], tile), lambda i, w: (0, i)) for x in flat],
                *[pl.BlockSpec(memory_space=pl.ANY) for _ in extra],
            ],
            out_specs=[
                pl.BlockSpec((rows, tile), row_block),
                pl.BlockSpec((rows, width), lambda i, w: (0, 0)),
            ],
            scratch_shapes=[
                pltpu.VMEM((2 * width, tile), jnp.bfloat16),
                pltpu.VMEM((rows, width), jnp.float32),
            ],
        ),
        out_shape=[
            jax.ShapeDtypeStruct(pre_act.shape, jnp.bfloat16),
            jax.ShapeDtypeStruct((rows, width), jnp.bfloat16),
        ],
        input_output_aliases={3 + len(flat): 0} if extra else {},
        compiler_params=pltpu.CompilerParams(vmem_limit_bytes=48 << 20),
        cost_estimate=SMALL,
        name="feed_rows",
    )(where, low, pre_act, *flat, *extra)


def whole_weights(pieces, width):
    chips, cores = lax.axis_size("seq"), lax.axis_size("sub")
    shard, units = pieces[0][1][0].shape
    places = [lax.axis_index(name) for name in ("seq", "sub", "groups")]
    whole = jnp.zeros((2 * width, units), jnp.bfloat16)
    for key, arrays in pieces:
        for at, x in zip(piece_rows(key, width, shard, *places, chips, cores), arrays):
            whole = lax.dynamic_update_slice_in_dim(whole, x, at, 0)
    return whole


def local(z_mix, z_ffn, pre_act, grad_out, gain_mix, gain_ffn, w_in, w_out):
    tok_rows, width = z_mix.shape
    unit_count = pre_act.shape[1]
    hids = lax.axis_size("hid")
    hid_index = lax.axis_index("hid")
    cores = lax.axis_size("sub")
    chips = lax.axis_size("seq")
    spans = chips * cores
    team = spans * hids
    half = width // 2
    slots = -(-half // team)
    rows = tok_rows // hids
    col_count = width // hids
    seq_length = tok_rows * spans
    shard_rows = w_in.shape[0]
    bf16 = jnp.bfloat16
    contract_units = (((1,), (1,)), ((), ()))
    contract_rows = (((0,), (0,)), ((), ()))

    def row_part(values, index):
        return lax.dynamic_slice_in_dim(values, index * rows, rows, 0)

    where = jnp.stack([lax.axis_index(name) for name in ("hid", "seq", "sub", "groups")])

    feats = jnp.arange(width, dtype=jnp.int32)
    core_ids = (lax.axis_index("sub") + jnp.arange(cores, dtype=jnp.int32)) % cores
    core_order = (
        jnp.arange(chips, dtype=jnp.int32)[None, :, None] * cores + core_ids[:, None, None]
    ) * shard_rows + jnp.arange(shard_rows, dtype=jnp.int32)[None, None]
    core_reorder = (feats[:, None] == core_order.reshape(1, width)).astype(bf16)

    ffn_grad, ffn_low = ffn_norm(z_ffn, grad_out, gain_ffn)
    pieces, arrived = weight_pieces(w_out, w_in, (ffn_low,))

    def core_rows(left, right, core):
        part = left[:, core * (width // cores) : (core + 1) * (width // cores)]
        return lax.dot_general(part, right, contract_rows, preferred_element_type=jnp.float32)

    def others_rows(left, right):
        return [core_rows(left, right, core).astype(bf16) for core in range(1, cores)]

    def chip_sum(left, right, sent):
        total = core_rows(left, right, 0)
        for core, part in enumerate(sent, 1):
            total += lax.ppermute(part, "sub", shift_pairs(cores, core)).astype(jnp.float32)
        return total.astype(bf16)

    def over_chips(total):
        return lax.psum_scatter(total, "seq", scatter_dimension=0, tiled=True).astype(jnp.float32)

    activation = lax.optimization_barrier(gelu_tanh(pre_act.astype(jnp.float32)).astype(bf16))
    total_out = lax.dot_general(ffn_low, activation, contract_rows, preferred_element_type=jnp.float32)
    total_out, *_ = lax.optimization_barrier((total_out.astype(bf16), *arrived[-1]))
    grad_w_out = lax.psum_scatter(total_out, SPANS, scatter_dimension=0, tiled=True).astype(jnp.float32)
    partials = []
    if shard_rows % 16 == 0 and rows % 16 == 0 and unit_count % 128 == 0:
        pre_grad = None
        for step in [*range(1, hids), 0]:
            pre_grad, part = feed_rows(where, ffn_low, pre_act, pieces, rows, step, pre_grad)
            partials.append(part)
    else:
        whole = whole_weights(pieces, width)
        act_grad = jnp.dot(ffn_low, whole[:width], preferred_element_type=jnp.float32)
        pre_grad = (gelu_slope(pre_act) * act_grad).astype(bf16)
        product = lax.dot_general(
            pre_grad, whole[width:], contract_units, preferred_element_type=jnp.float32
        ).astype(bf16)
        for step in [*range(1, hids), 0]:
            partials.append(row_part(product, (hid_index + step) % hids))

    seed = jnp.zeros((), jnp.int32)
    late_z, seed, *_ = lax.optimization_barrier((z_mix, seed, *partials[:-1]))
    normed_core = mix_norm(late_z, gain_mix, core_reorder)
    feat_tab = lax.optimization_barrier(feature_table(feats + seed, seed, width, slots, team))

    parts = [partials.pop()]
    for step, part in enumerate(partials, 1):
        parts.append(lax.ppermute(part, "hid", shift_pairs(hids, step)))
    sent = others_rows(normed_core, pre_grad)
    feat_tab, *_ = lax.optimization_barrier((feat_tab, *sent))
    mix_low, spectral = mix_rows(where, z_mix, ffn_grad, gain_mix, feat_tab, parts, hids)

    pre_grad, seed, spectral = lax.optimization_barrier((pre_grad, seed, spectral))
    pos_tab = lax.optimization_barrier(position_table(tok_rows, seed))
    t_cos, t_sin = turn(
        (jnp.arange(spans, dtype=jnp.int32) + seed)[:, None] * (jnp.arange(tok_rows, dtype=jnp.int32) + seed)[None],
        seq_length,
    )
    twist = jnp.stack([t_cos, t_sin]) * (1.0 / math.sqrt(seq_length * width))
    team_index = lax.axis_index(TEAM)
    mark = ((team_index * slots + jnp.arange(slots, dtype=jnp.int32)) == seed).astype(jnp.float32)[:, None]
    own_ids = hid_index * col_count + jnp.arange(col_count, dtype=jnp.int32) + seed
    own_slot = jnp.where(own_ids < half, own_ids, jnp.where(own_ids == half, 0, width - own_ids))
    pick = (jnp.arange(team * slots, dtype=jnp.int32)[:, None] == own_slot[None]).astype(bf16)

    grad_w_in = over_chips(chip_sum(normed_core, pre_grad, sent))
    got = lax.all_to_all(
        spectral.reshape(team, 2 * slots, rows), TEAM, split_axis=0, concat_axis=0, tiled=True
    )
    def col_part(values, index):
        return lax.dynamic_slice_in_dim(values, index * col_count, col_count, 1)

    own = jnp.zeros((tok_rows, col_count), bf16)
    own = lax.dynamic_update_slice_in_dim(own, col_part(mix_low, hid_index), hid_index * rows, 0)
    for step in range(1, hids):
        sent = col_part(mix_low, (hid_index + step) % hids)
        came = lax.ppermute(sent, "hid", shift_pairs(hids, step))
        own = lax.dynamic_update_slice_in_dim(own, came, (hid_index - step) % hids * rows, 0)
    got, own, grad_w_out = lax.optimization_barrier((got, own, grad_w_out))
    sent_back = position_transform(got, mark, twist, pos_tab, spans, hids, slots)
    back = lax.all_to_all(sent_back, TEAM, split_axis=0, concat_axis=0, tiled=True)
    back, grad_w_in, grad_w_out = lax.optimization_barrier((back, grad_w_in, grad_w_out))
    grad_in = finish(back, pick, own, spans, slots)
    return (grad_in, grad_w_in, grad_w_out)


def solution(mesh):
    in_specs = (
        P(("groups", "seq", "sub"), None),
        P(("groups", "seq", "sub"), None),
        P(("groups", "seq", "sub"), "hid"),
        P(("groups", "seq", "sub"), None),
        P(),
        P(),
        P(("seq", "sub"), "hid"),
        P(("seq", "sub"), "hid"),
    )
    out_specs = (
        P(("groups", "seq", "sub"), "hid"),
        P(("groups", "seq", "sub"), "hid"),
        P(("groups", "seq", "sub"), "hid"),
    )
    return jax.shard_map(local, mesh=mesh, in_specs=in_specs, out_specs=out_specs, check_vma=False)
```

```python
import functools
import math

import jax
import jax.numpy as jnp
from jax import lax
from jax.experimental import pallas as pl
from jax.experimental.pallas import tpu as pltpu
from jax.sharding import PartitionSpec as P

epsilon = 1e-05
SPANS = ("seq", "sub")
TEAM = ("seq", "sub", "hid")
LANES = 128
ROWS = 128
SMALL = pl.CostEstimate(flops=1 << 20, bytes_accessed=1 << 16, transcendentals=0)


def norm_parts(values):
    values = values.astype(jnp.float32)
    row_mean = jnp.mean(values, axis=-1, keepdims=True)
    centred = values - row_mean
    inv_std = lax.rsqrt(jnp.mean(centred * centred, axis=-1, keepdims=True) + epsilon)
    return (centred * inv_std, inv_std)


def norm_backward(values, gain_vec, upstream):
    unit_rows, inv_std = norm_parts(values)
    scaled = upstream * gain_vec
    return inv_std * (
        scaled
        - jnp.mean(scaled, axis=-1, keepdims=True)
        - unit_rows * jnp.mean(scaled * unit_rows, axis=-1, keepdims=True)
    )


def gelu_tanh(values):
    return jax.nn.gelu(values, approximate=True)


def shift_pairs(size, step):
    return [(i, (i + step) % size) for i in range(size)]


def turn(products, period):
    angles = (2.0 * math.pi / period) * (products % period).astype(jnp.float32)
    return (jnp.cos(angles), jnp.sin(angles))


def feature_table(feats, seed, width, slots, team):
    half = width // 2
    cos_a, sin_a = turn(slots * (jnp.arange(team, dtype=jnp.int32) + seed)[:, None] * feats[None], width)
    cos_b, sin_b = turn((jnp.arange(slots, dtype=jnp.int32) + seed)[:, None] * feats[None], width)
    slot = lax.broadcasted_iota(jnp.int32, (team, slots, 1), 0) * slots
    slot = slot + lax.broadcasted_iota(jnp.int32, (team, slots, 1), 1)
    cos_all = cos_a[:, None] * cos_b[None] - sin_a[:, None] * sin_b[None]
    sin_all = sin_a[:, None] * cos_b[None] + cos_a[:, None] * sin_b[None]
    top = (1 - 2 * (feats % 2)).astype(jnp.float32)[None, None]
    sin_all = jnp.where(slot == 0, top, sin_all)
    table = jnp.where(slot < half, jnp.stack([cos_all, sin_all], axis=1).transpose(1, 0, 2, 3), 0.0)
    return table.astype(jnp.bfloat16).transpose(1, 0, 2, 3).reshape(team * 2 * slots, width)


def position_table(count, seed):
    fine = 32
    coarse = count // fine
    col = jnp.arange(count, dtype=jnp.int32) + seed
    cos_a, sin_a = turn(fine * (jnp.arange(coarse, dtype=jnp.int32) + seed)[:, None] * col[None], count)
    cos_b, sin_b = turn((jnp.arange(fine, dtype=jnp.int32) + seed)[:, None] * col[None], count)
    cos_a, sin_a = cos_a[:, None], sin_a[:, None]
    cos_b, sin_b = cos_b[None], sin_b[None]
    both = jnp.stack([cos_a * cos_b - sin_a * sin_b, -sin_a * cos_b - cos_a * sin_b])
    return both.astype(jnp.bfloat16).reshape(2 * count, count)


def combine(terms):
    total = None
    for factor, value in terms:
        if abs(factor) < 1e-12:
            continue
        if abs(factor - 1.0) < 1e-12:
            total = value if total is None else total + value
        elif abs(factor + 1.0) < 1e-12:
            total = -value if total is None else total - value
        else:
            part = factor * value
            total = part if total is None else total + part
    return total


def span_transform(parts, freq, spans):
    angles = [2.0 * math.pi * (r * freq % spans) / spans for r in range(spans)]
    real = combine([(math.cos(a), p) for a, p in zip(angles, parts)])
    imag = combine([(math.sin(a), p) for a, p in zip(angles, parts)])
    return (real, imag)


def position_kernel(spans, hids, slots, x_ref, mark_ref, twist_ref, tab_ref, o_ref, v_ref):
    rows_in = x_ref.shape[2]
    count = rows_in * hids
    own_rows = spans * slots

    @pl.when(pl.program_id(0) == 0)
    def _():
        mark = jnp.broadcast_to(mark_ref[...], (slots, LANES)) > 0.5
        for hid in range(hids):
            for piece in range(rows_in // LANES):
                lanes = slice(piece * LANES, (piece + 1) * LANES)
                at = hid * rows_in + piece * LANES
                blocks = [x_ref[r * hids + hid, :, lanes].astype(jnp.float32) for r in range(spans)]
                cos_parts = [b[:slots] for b in blocks]
                sin_parts = [b[slots:] for b in blocks]
                cos_half, sin_half = [], []
                for freq in range(spans // 2 + 1):
                    cos_half.append(span_transform(cos_parts, freq, spans))
                    sin_half.append(span_transform(sin_parts, freq, spans))
                held = []
                for freq in range(spans):
                    low = min(freq, spans - freq)
                    c_re, c_im = cos_half[low]
                    s_re, s_im = sin_half[low]
                    if c_im is None:
                        c_im, s_im = jnp.zeros_like(c_re), jnp.zeros_like(s_re)
                    elif low != freq:
                        c_im, s_im = -c_im, -s_im
                    t_re = jnp.broadcast_to(twist_ref[0, freq : freq + 1, at : at + LANES], c_re.shape)
                    t_im = jnp.broadcast_to(twist_ref[1, freq : freq + 1, at : at + LANES], c_re.shape)
                    pairs = (
                        (jnp.where(mark, c_re, c_re - s_im), jnp.where(mark, c_im, c_im + s_re)),
                        (jnp.where(mark, s_re, c_re + s_im), jnp.where(mark, s_im, c_im - s_re)),
                    )
                    held.append(
                        [(re * t_re - im * t_im, re * t_im + im * t_re) for re, im in pairs]
                    )
                    if freq % 2 == 1:
                        row = (freq - 1) * slots
                        for side in range(2):
                            for part in range(2):
                                v_ref[
                                    side * own_rows + row : side * own_rows + row + 2 * slots,
                                    part * count + at : part * count + at + LANES,
                                ] = jnp.concatenate(
                                    [held[0][side][part], held[1][side][part]], axis=0
                                ).astype(v_ref.dtype)
                        held = []

    res = jnp.dot(v_ref[...], tab_ref[...], preferred_element_type=jnp.float32)
    res = res.astype(o_ref.dtype)
    for dest in range(o_ref.shape[0]):
        for side in range(2):
            o_ref[dest, side] = res[
                side * own_rows : (side + 1) * own_rows, dest * LANES : (dest + 1) * LANES
            ]


def position_transform(got, mark, twist, table, spans, hids, slots):
    count = table.shape[1]
    share = count // spans
    team = spans * hids
    rows = spans * slots
    if hids == 2 and share == LANES and slots % 8 == 0 and spans % 2 == 0:
        dests = 4 if spans % 4 == 0 else 2
        out = pl.pallas_call(
            functools.partial(position_kernel, spans, hids, slots),
            grid=(spans // dests,),
            in_specs=[
                pl.BlockSpec(got.shape, lambda i: (0, 0, 0)),
                pl.BlockSpec(mark.shape, lambda i: (0, 0)),
                pl.BlockSpec(twist.shape, lambda i: (0, 0, 0)),
                pl.BlockSpec((2 * count, dests * LANES), lambda i: (0, i)),
            ],
            out_specs=pl.BlockSpec((dests, hids, rows, LANES), lambda i: (i, 0, 0, 0)),
            out_shape=jax.ShapeDtypeStruct((spans, hids, rows, LANES), jnp.bfloat16),
            scratch_shapes=[pltpu.VMEM((2 * rows, 2 * count), jnp.bfloat16)],
            compiler_params=pltpu.CompilerParams(vmem_limit_bytes=58 << 20),
            cost_estimate=pl.CostEstimate(
                flops=2 * 2 * rows * 2 * count * count, bytes_accessed=6 << 20, transcendentals=0
            ),
            name="position_transform",
        )(got, mark, twist, table)
        return out.reshape(team, rows, share)
    wide = got.astype(jnp.float32).reshape(spans, hids, 2, slots, count // hids)
    wide = wide.transpose(2, 0, 3, 1, 4).reshape(2, spans, slots, count)
    ids = jnp.arange(spans, dtype=jnp.int32)
    cos_s, sin_s = turn(ids[:, None] * ids[None], spans)
    exact = lax.Precision.HIGHEST
    re = jnp.einsum("kr,crsn->cksn", cos_s, wide, precision=exact)
    im = jnp.einsum("kr,crsn->cksn", sin_s, wide, precision=exact)
    special = mark > 0.5
    v_re = jnp.stack([jnp.where(special, re[0], re[0] - im[1]), jnp.where(special, re[1], re[0] + im[1])])
    v_im = jnp.stack([jnp.where(special, im[0], im[0] + re[1]), jnp.where(special, im[1], im[0] - re[1])])
    t_re, t_im = twist[0][:, None], twist[1][:, None]
    both = jnp.concatenate([v_re * t_re - v_im * t_im, v_re * t_im + v_im * t_re], axis=-1)
    res = jnp.dot(
        both.astype(jnp.bfloat16).reshape(2 * rows, 2 * count), table, preferred_element_type=jnp.float32
    ).astype(jnp.bfloat16)
    res = res.reshape(2, rows, spans, share).transpose(2, 0, 1, 3)
    res = jnp.repeat(res, hids // 2, axis=1)
    return res.reshape(team, rows, share)


def finish_kernel(spans, slots, back_ref, pick_ref, own_ref, o_ref, held_ref):
    team = back_ref.shape[0]
    groups = held_ref.shape[0]
    for freq in range(spans):
        rows = slice(freq * slots, (freq + 1) * slots)
        block = jnp.concatenate(
            [back_ref[s].astype(jnp.float32)[rows] for s in range(team)], axis=0
        ).astype(jnp.bfloat16)
        value = lax.dot_general(
            block, pick_ref[...], (((0,), (0,)), ((), ())), preferred_element_type=jnp.float32
        )
        for g in range(groups):
            held_ref[g, pl.ds(freq, LANES, stride=spans), :] = value[:, g * LANES : (g + 1) * LANES]
    for g in range(groups):
        lanes = slice(g * LANES, (g + 1) * LANES)
        o_ref[:, lanes] = own_ref[:, lanes] + held_ref[g]


def finish(back, pick, own, spans, slots):
    team, rows, share = back.shape
    if share == LANES and slots % 8 == 0 and own.shape[1] % LANES == 0:
        return pl.pallas_call(
            functools.partial(finish_kernel, spans, slots),
            out_shape=jax.ShapeDtypeStruct(own.shape, jnp.float32),
            scratch_shapes=[pltpu.VMEM((own.shape[1] // LANES, own.shape[0], LANES), jnp.float32)],
            compiler_params=pltpu.CompilerParams(vmem_limit_bytes=48 << 20),
            cost_estimate=pl.CostEstimate(
                flops=2 * own.shape[0] * pick.size, bytes_accessed=5 << 20, transcendentals=0
            ),
            name="finish",
        )(back, pick, own)
    value = jnp.einsum(
        "skjn,sjm->nkm",
        back.reshape(team, spans, slots, share),
        pick.reshape(team, slots, pick.shape[1]),
        preferred_element_type=jnp.float32,
    )
    return own + value.reshape(own.shape)


def ffn_norm_kernel(z_ref, up_ref, gain_ref, grad_ref, low_ref):
    grad = norm_backward(z_ref[...], gain_ref[...], up_ref[...].astype(jnp.float32))
    low = grad.astype(jnp.bfloat16)
    grad_ref[...] = grad
    low_ref[...] = low


def ffn_norm(z_ffn, grad_out, gain):
    rows, width = z_ffn.shape
    tile = pl.BlockSpec((ROWS, width), lambda i: (i, 0))
    return pl.pallas_call(
        ffn_norm_kernel,
        grid=(rows // ROWS,),
        in_specs=[tile, tile, pl.BlockSpec((1, width), lambda i: (0, 0))],
        out_specs=[tile, tile],
        out_shape=[
            jax.ShapeDtypeStruct(z_ffn.shape, jnp.float32),
            jax.ShapeDtypeStruct(z_ffn.shape, jnp.bfloat16),
        ],
        compiler_params=pltpu.CompilerParams(vmem_limit_bytes=32 << 20),
        cost_estimate=SMALL,
        name="ffn_norm",
    )(z_ffn, grad_out, gain[None])


def mix_norm_kernel(z_ref, gain_ref, order_ref, core_ref):
    normed = (norm_parts(z_ref[...])[0] * gain_ref[...]).astype(jnp.bfloat16)
    core_ref[...] = jnp.dot(normed, order_ref[...], preferred_element_type=jnp.float32).astype(jnp.bfloat16)


def mix_norm(z_mix, gain, order):
    rows, width = z_mix.shape
    tile = pl.BlockSpec((ROWS, width), lambda i: (i, 0))
    return pl.pallas_call(
        mix_norm_kernel,
        grid=(rows // ROWS,),
        in_specs=[tile, pl.BlockSpec((1, width), lambda i: (0, 0)), pl.BlockSpec(order.shape, lambda i: (0, 0))],
        out_specs=tile,
        out_shape=jax.ShapeDtypeStruct(z_mix.shape, jnp.bfloat16),
        compiler_params=pltpu.CompilerParams(vmem_limit_bytes=32 << 20),
        cost_estimate=SMALL,
        name="mix_norm",
    )(z_mix, gain[None], order)


def gelu_slope(values):
    scale = math.sqrt(2.0 / math.pi)
    a = values.astype(jnp.float32)
    square = a * a
    tanh = jnp.tanh(scale * a * (1.0 + 0.044715 * square))
    upper = 0.5 * (1.0 + tanh)
    return upper + (0.5 * scale) * a * (1.0 - tanh * tanh) * (1.0 + (3.0 * 0.044715) * square)


def slope_kernel(where_ref, pre_act_ref, slope_ref):
    slope_ref[...] = gelu_slope(pre_act_ref[...])


def slope_rows(where, pre_act, rows, step):
    hids, units = lax.axis_size("hid"), pre_act.shape[1]
    steps = rows // ROWS
    return pl.pallas_call(
        slope_kernel,
        grid_spec=pltpu.PrefetchScalarGridSpec(
            num_scalar_prefetch=1,
            grid=(steps,),
            in_specs=[pl.BlockSpec((ROWS, units), lambda i, w: (lax.rem(w[0] + step, hids) * steps + i, 0))],
            out_specs=pl.BlockSpec((ROWS, units), lambda i, w: (i, 0)),
        ),
        out_shape=jax.ShapeDtypeStruct((rows, units), jnp.float32),
        compiler_params=pltpu.CompilerParams(vmem_limit_bytes=32 << 20),
        cost_estimate=SMALL,
        name="slope_rows",
    )(where, pre_act)


def mix_kernel(count, hids, where_ref, z_ref, ffn_ref, gain_ref, tab_ref, *refs):
    parts, (mix_ref, spec_ref) = refs[:count], refs[count:]
    summed = parts[0][...].astype(jnp.float32)
    for part in parts[1:]:
        summed += part[...].astype(jnp.float32)
    mix = norm_backward(z_ref[...], gain_ref[...], ffn_ref[...] + summed)
    low = mix.astype(jnp.bfloat16)
    mix_ref[...] = low
    spec_ref[...] = lax.dot_general(
        tab_ref[...], low, (((1,), (1,)), ((), ())), preferred_element_type=jnp.float32
    ).astype(jnp.bfloat16)


def mix_rows(where, z_mix, ffn_grad, gain, table, parts, hids):
    rows, width = parts[0].shape
    size = min(rows, 256)
    steps = rows // size
    tile = pl.BlockSpec((size, width), lambda i, w: (i, 0))
    own = pl.BlockSpec((size, width), lambda i, w: (w[0] * steps + i, 0))
    return pl.pallas_call(
        functools.partial(mix_kernel, len(parts), hids),
        grid_spec=pltpu.PrefetchScalarGridSpec(
            num_scalar_prefetch=1,
            grid=(steps,),
            in_specs=[
                own,
                own,
                pl.BlockSpec((1, width), lambda i, w: (0, 0)),
                pl.BlockSpec(table.shape, lambda i, w: (0, 0)),
                *[tile for _ in parts],
            ],
            out_specs=[tile, pl.BlockSpec((table.shape[0], size), lambda i, w: (0, i))],
        ),
        out_shape=[
            jax.ShapeDtypeStruct((rows, width), jnp.bfloat16),
            jax.ShapeDtypeStruct((table.shape[0], rows), jnp.bfloat16),
        ],
        compiler_params=pltpu.CompilerParams(vmem_limit_bytes=32 << 20),
        cost_estimate=SMALL,
        name="mix_rows",
    )(where, z_mix, ffn_grad, gain[None], table, *parts)


def weight_pieces(w_out, w_in, first, during):
    chips, cores, groups = (lax.axis_size(name) for name in ("seq", "sub", "groups"))
    mine = [w_out, w_in]
    if groups == 2:
        mine = [jnp.where(lax.axis_index("groups") == 0, w_out, w_in)]
    near = [((0, 0), (w_out, w_in))]
    steps = sorted(range(1, chips), key=lambda d: (min(d, chips - d), d))
    waves = [steps[k : k + 2] for k in range(0, len(steps), 2)]
    arrived = []
    for wave in waves:
        if arrived:
            mine = lax.optimization_barrier((tuple(mine), arrived[-1], first))[0]
        came = [tuple(lax.ppermute(w, "seq", shift_pairs(chips, d)) for w in mine) for d in wave]
        held = [i for i, ((d, k), _) in enumerate(near) if k == 1]
        if held:
            came, ready, during = lax.optimization_barrier((came, [near[i][1] for i in held], during))
            for i, arrays in zip(held, ready):
                near[i] = (near[i][0], arrays)
        arrived.append([x for blocks in came for x in blocks])
        for d, blocks in zip(wave, came):
            near.append(((d, 0), blocks))
            if groups == 2:
                near.append(((d, 1), (lax.ppermute(blocks[0], "groups", shift_pairs(2, 1)),)))
    pieces = [((0, d, k), arrays) for (d, k), arrays in near]
    for e in range(1, cores):
        for (d, k), arrays in near:
            pieces.append(
                ((e, d, k), tuple(lax.ppermute(x, "sub", shift_pairs(cores, -e)) for x in arrays))
            )
    return pieces, arrived, during


def piece_rows(key, width, shard, seq, sub, group, chips, cores):
    e, d, k = key
    row = (lax.rem(seq + chips - d, chips) * cores + lax.rem(sub + e, cores)) * shard
    if d and lax.axis_size("groups") == 2:
        return [row + lax.rem(group + k, 2) * width]
    return [row, row + width]


def feed_kernel(keys, count, shard, chips, cores, carried, ready, where_ref, x_ref, pre_act_ref, *refs):
    blocks, refs = list(refs[:count]), refs[count + carried :]
    pre_ref, part_ref, weights, total = refs
    width = x_ref.shape[1]
    for key in keys:
        for at in piece_rows(key, width, shard, where_ref[1], where_ref[2], where_ref[3], chips, cores):
            weights[pl.ds(pl.multiple_of(at, shard), shard), :] = blocks.pop(0)[...]
    act_grad = jnp.dot(x_ref[...], weights[:width, :], preferred_element_type=jnp.float32)
    slope = pre_act_ref[...] if ready else gelu_slope(pre_act_ref[...])
    pre_grad = (slope * act_grad).astype(jnp.bfloat16)
    pre_ref[...] = pre_grad
    term = lax.dot_general(
        pre_grad, weights[width:, :], (((1,), (1,)), ((), ())), preferred_element_type=jnp.float32
    )
    first = pl.program_id(0) == 0

    @pl.when(first)
    def _():
        total[...] = term

    @pl.when(jnp.logical_not(first))
    def _():
        total[...] += term

    @pl.when(pl.program_id(0) == pl.num_programs(0) - 1)
    def _():
        part_ref[...] = total[...].astype(part_ref.dtype)


def feed_rows(where, low, pre_act, pieces, rows, step, carried, slope=None):
    chips, cores, hids = (lax.axis_size(name) for name in ("seq", "sub", "hid"))
    width, units = low.shape[1], pre_act.shape[1]
    shard = pieces[0][1][0].shape[0]
    tile = 768 if units % 768 == 0 else 128
    keys = [key for key, _ in pieces]
    flat = [x for _, arrays in pieces for x in arrays]

    def row_block(i, where_ref):
        return (lax.rem(where_ref[0] + step, hids), i)

    extra = [] if carried is None else [carried]
    return pl.pallas_call(
        functools.partial(feed_kernel, keys, len(flat), shard, chips, cores, len(extra), slope is not None),
        grid_spec=pltpu.PrefetchScalarGridSpec(
            num_scalar_prefetch=1,
            grid=(units // tile,),
            in_specs=[
                pl.BlockSpec((rows, width), lambda i, w: (lax.rem(w[0] + step, hids), 0)),
                pl.BlockSpec((rows, tile), row_block if slope is None else lambda i, w: (0, i)),
                *[pl.BlockSpec((x.shape[0], tile), lambda i, w: (0, i)) for x in flat],
                *[pl.BlockSpec(memory_space=pl.ANY) for _ in extra],
            ],
            out_specs=[
                pl.BlockSpec((rows, tile), row_block),
                pl.BlockSpec((rows, width), lambda i, w: (0, 0)),
            ],
            scratch_shapes=[
                pltpu.VMEM((2 * width, tile), jnp.bfloat16),
                pltpu.VMEM((rows, width), jnp.float32),
            ],
        ),
        out_shape=[
            jax.ShapeDtypeStruct(pre_act.shape, jnp.bfloat16),
            jax.ShapeDtypeStruct((rows, width), jnp.bfloat16),
        ],
        input_output_aliases={3 + len(flat): 0} if extra else {},
        compiler_params=pltpu.CompilerParams(vmem_limit_bytes=60 << 20),
        cost_estimate=SMALL,
        name="feed_rows",
    )(where, low, pre_act if slope is None else slope, *flat, *extra)


def whole_weights(pieces, width):
    chips, cores = lax.axis_size("seq"), lax.axis_size("sub")
    shard, units = pieces[0][1][0].shape
    places = [lax.axis_index(name) for name in ("seq", "sub", "groups")]
    whole = jnp.zeros((2 * width, units), jnp.bfloat16)
    for key, arrays in pieces:
        for at, x in zip(piece_rows(key, width, shard, *places, chips, cores), arrays):
            whole = lax.dynamic_update_slice_in_dim(whole, x, at, 0)
    return whole


def local(z_mix, z_ffn, pre_act, grad_out, gain_mix, gain_ffn, w_in, w_out):
    tok_rows, width = z_mix.shape
    unit_count = pre_act.shape[1]
    hids = lax.axis_size("hid")
    hid_index = lax.axis_index("hid")
    cores = lax.axis_size("sub")
    chips = lax.axis_size("seq")
    spans = chips * cores
    team = spans * hids
    half = width // 2
    slots = -(-half // team)
    rows = tok_rows // hids
    col_count = width // hids
    seq_length = tok_rows * spans
    shard_rows = w_in.shape[0]
    bf16 = jnp.bfloat16
    contract_units = (((1,), (1,)), ((), ()))
    contract_rows = (((0,), (0,)), ((), ()))

    def row_part(values, index):
        return lax.dynamic_slice_in_dim(values, index * rows, rows, 0)

    where = jnp.stack([lax.axis_index(name) for name in ("hid", "seq", "sub", "groups")])

    feats = jnp.arange(width, dtype=jnp.int32)
    core_ids = (lax.axis_index("sub") + jnp.arange(cores, dtype=jnp.int32)) % cores
    core_order = (
        jnp.arange(chips, dtype=jnp.int32)[None, :, None] * cores + core_ids[:, None, None]
    ) * shard_rows + jnp.arange(shard_rows, dtype=jnp.int32)[None, None]
    core_reorder = (feats[:, None] == core_order.reshape(1, width)).astype(bf16)

    ffn_grad, ffn_low = ffn_norm(z_ffn, grad_out, gain_ffn)
    fast = shard_rows % 16 == 0 and rows % ROWS == 0 and unit_count % 128 == 0
    slopes = [slope_rows(where, pre_act, rows, step) for step in range(1, hids)] if fast else []
    pieces, arrived, (normed_core, slopes) = weight_pieces(
        w_out, w_in, (ffn_low,), (mix_norm(z_mix, gain_mix, core_reorder), slopes)
    )

    def core_rows(left, right, core):
        part = left[:, core * (width // cores) : (core + 1) * (width // cores)]
        return lax.dot_general(part, right, contract_rows, preferred_element_type=jnp.float32)

    def others_rows(left, right):
        return [core_rows(left, right, core).astype(bf16) for core in range(1, cores)]

    def chip_sum(left, right, sent):
        total = core_rows(left, right, 0)
        for core, part in enumerate(sent, 1):
            total += lax.ppermute(part, "sub", shift_pairs(cores, core)).astype(jnp.float32)
        return total.astype(bf16)

    def over_chips(total):
        return lax.psum_scatter(total, "seq", scatter_dimension=0, tiled=True).astype(jnp.float32)

    activation = lax.optimization_barrier(gelu_tanh(pre_act.astype(jnp.float32)).astype(bf16))
    total_out = lax.dot_general(ffn_low, activation, contract_rows, preferred_element_type=jnp.float32)
    total_out, *_ = lax.optimization_barrier((total_out.astype(bf16), *arrived[-1]))
    grad_w_out = lax.psum_scatter(total_out, SPANS, scatter_dimension=0, tiled=True).astype(jnp.float32)
    partials = []
    if fast:
        pre_grad = None
        for step in [*range(1, hids), 0]:
            slope = slopes[step - 1] if step else None
            pre_grad, part = feed_rows(where, ffn_low, pre_act, pieces, rows, step, pre_grad, slope)
            partials.append(part)
    else:
        whole = whole_weights(pieces, width)
        act_grad = jnp.dot(ffn_low, whole[:width], preferred_element_type=jnp.float32)
        pre_grad = (gelu_slope(pre_act) * act_grad).astype(bf16)
        product = lax.dot_general(
            pre_grad, whole[width:], contract_units, preferred_element_type=jnp.float32
        ).astype(bf16)
        for step in [*range(1, hids), 0]:
            partials.append(row_part(product, (hid_index + step) % hids))

    seed = jnp.zeros((), jnp.int32)
    seed, *_ = lax.optimization_barrier((seed, *partials[:-1]))
    feat_tab = lax.optimization_barrier(feature_table(feats + seed, seed, width, slots, team))

    parts = [partials.pop()]
    for step, part in enumerate(partials, 1):
        parts.append(lax.ppermute(part, "hid", shift_pairs(hids, step)))
    sent = others_rows(normed_core, pre_grad)
    feat_tab, *_ = lax.optimization_barrier((feat_tab, *sent))
    mix_low, spectral = mix_rows(where, z_mix, ffn_grad, gain_mix, feat_tab, parts, hids)

    pre_grad, seed, spectral = lax.optimization_barrier((pre_grad, seed, spectral))
    grad_w_in = over_chips(chip_sum(normed_core, pre_grad, sent))
    pos_tab = lax.optimization_barrier(position_table(tok_rows, seed))
    t_cos, t_sin = turn(
        (jnp.arange(spans, dtype=jnp.int32) + seed)[:, None] * (jnp.arange(tok_rows, dtype=jnp.int32) + seed)[None],
        seq_length,
    )
    twist = jnp.stack([t_cos, t_sin]) * (1.0 / math.sqrt(seq_length * width))
    team_index = lax.axis_index(TEAM)
    mark = ((team_index * slots + jnp.arange(slots, dtype=jnp.int32)) == seed).astype(jnp.float32)[:, None]
    own_ids = hid_index * col_count + jnp.arange(col_count, dtype=jnp.int32) + seed
    own_slot = jnp.where(own_ids < half, own_ids, jnp.where(own_ids == half, 0, width - own_ids))
    pick = (jnp.arange(team * slots, dtype=jnp.int32)[:, None] == own_slot[None]).astype(bf16)

    got = lax.all_to_all(
        spectral.reshape(team, 2 * slots, rows), TEAM, split_axis=0, concat_axis=0, tiled=True
    )
    def col_part(values, index):
        return lax.dynamic_slice_in_dim(values, index * col_count, col_count, 1)

    own = jnp.zeros((tok_rows, col_count), bf16)
    own = lax.dynamic_update_slice_in_dim(own, col_part(mix_low, hid_index), hid_index * rows, 0)
    for step in range(1, hids):
        sent = col_part(mix_low, (hid_index + step) % hids)
        came = lax.ppermute(sent, "hid", shift_pairs(hids, step))
        own = lax.dynamic_update_slice_in_dim(own, came, (hid_index - step) % hids * rows, 0)
    got, own, grad_w_out = lax.optimization_barrier((got, own, grad_w_out))
    sent_back = position_transform(got, mark, twist, pos_tab, spans, hids, slots)
    back = lax.all_to_all(sent_back, TEAM, split_axis=0, concat_axis=0, tiled=True)
    back, grad_w_in, grad_w_out = lax.optimization_barrier((back, grad_w_in, grad_w_out))
    grad_in = finish(back, pick, own, spans, slots)
    return (grad_in, grad_w_in, grad_w_out)


def solution(mesh):
    in_specs = (
        P(("groups", "seq", "sub"), None),
        P(("groups", "seq", "sub"), None),
        P(("groups", "seq", "sub"), "hid"),
        P(("groups", "seq", "sub"), None),
        P(),
        P(),
        P(("seq", "sub"), "hid"),
        P(("seq", "sub"), "hid"),
    )
    out_specs = (
        P(("groups", "seq", "sub"), "hid"),
        P(("groups", "seq", "sub"), "hid"),
        P(("groups", "seq", "sub"), "hid"),
    )
    return jax.shard_map(local, mesh=mesh, in_specs=in_specs, out_specs=out_specs, check_vma=False)
```

```python
import functools
import math

import jax
import jax.numpy as jnp
from jax import lax
from jax.experimental import pallas as pl
from jax.experimental.pallas import tpu as pltpu
from jax.sharding import PartitionSpec as P

epsilon = 1e-05
SPANS = ("seq", "sub")
TEAM = ("seq", "sub", "hid")
LANES = 128
ROWS = 128
SMALL = pl.CostEstimate(flops=1 << 20, bytes_accessed=1 << 16, transcendentals=0)


def norm_parts(values):
    values = values.astype(jnp.float32)
    row_mean = jnp.mean(values, axis=-1, keepdims=True)
    centred = values - row_mean
    inv_std = lax.rsqrt(jnp.mean(centred * centred, axis=-1, keepdims=True) + epsilon)
    return (centred * inv_std, inv_std)


def norm_backward(values, gain_vec, upstream):
    unit_rows, inv_std = norm_parts(values)
    scaled = upstream * gain_vec
    return inv_std * (
        scaled
        - jnp.mean(scaled, axis=-1, keepdims=True)
        - unit_rows * jnp.mean(scaled * unit_rows, axis=-1, keepdims=True)
    )


def gelu_tanh(values):
    return jax.nn.gelu(values, approximate=True)


def shift_pairs(size, step):
    return [(i, (i + step) % size) for i in range(size)]


def turn(products, period):
    angles = (2.0 * math.pi / period) * (products % period).astype(jnp.float32)
    return (jnp.cos(angles), jnp.sin(angles))


def feature_table(feats, seed, width, slots, team):
    half = width // 2
    cos_a, sin_a = turn(slots * (jnp.arange(team, dtype=jnp.int32) + seed)[:, None] * feats[None], width)
    cos_b, sin_b = turn((jnp.arange(slots, dtype=jnp.int32) + seed)[:, None] * feats[None], width)
    slot = lax.broadcasted_iota(jnp.int32, (team, slots, 1), 0) * slots
    slot = slot + lax.broadcasted_iota(jnp.int32, (team, slots, 1), 1)
    cos_all = cos_a[:, None] * cos_b[None] - sin_a[:, None] * sin_b[None]
    sin_all = sin_a[:, None] * cos_b[None] + cos_a[:, None] * sin_b[None]
    top = (1 - 2 * (feats % 2)).astype(jnp.float32)[None, None]
    sin_all = jnp.where(slot == 0, top, sin_all)
    table = jnp.where(slot < half, jnp.stack([cos_all, sin_all], axis=1).transpose(1, 0, 2, 3), 0.0)
    return table.astype(jnp.bfloat16).transpose(1, 0, 2, 3).reshape(team * 2 * slots, width)


def position_table(count, seed):
    fine = 32
    coarse = count // fine
    col = jnp.arange(count, dtype=jnp.int32) + seed
    cos_a, sin_a = turn(fine * (jnp.arange(coarse, dtype=jnp.int32) + seed)[:, None] * col[None], count)
    cos_b, sin_b = turn((jnp.arange(fine, dtype=jnp.int32) + seed)[:, None] * col[None], count)
    cos_a, sin_a = cos_a[:, None], sin_a[:, None]
    cos_b, sin_b = cos_b[None], sin_b[None]
    both = jnp.stack([cos_a * cos_b - sin_a * sin_b, -sin_a * cos_b - cos_a * sin_b])
    return both.astype(jnp.bfloat16).reshape(2 * count, count)


def combine(terms):
    total = None
    for factor, value in terms:
        if abs(factor) < 1e-12:
            continue
        if abs(factor - 1.0) < 1e-12:
            total = value if total is None else total + value
        elif abs(factor + 1.0) < 1e-12:
            total = -value if total is None else total - value
        else:
            part = factor * value
            total = part if total is None else total + part
    return total


def span_transform(parts, freq, spans):
    angles = [2.0 * math.pi * (r * freq % spans) / spans for r in range(spans)]
    real = combine([(math.cos(a), p) for a, p in zip(angles, parts)])
    imag = combine([(math.sin(a), p) for a, p in zip(angles, parts)])
    return (real, imag)


def position_kernel(spans, hids, slots, x_ref, mark_ref, twist_ref, tab_ref, o_ref, v_ref):
    rows_in = x_ref.shape[2]
    count = rows_in * hids
    own_rows = spans * slots

    @pl.when(pl.program_id(0) == 0)
    def _():
        mark = jnp.broadcast_to(mark_ref[...], (slots, LANES)) > 0.5
        for hid in range(hids):
            for piece in range(rows_in // LANES):
                lanes = slice(piece * LANES, (piece + 1) * LANES)
                at = hid * rows_in + piece * LANES
                blocks = [x_ref[r * hids + hid, :, lanes].astype(jnp.float32) for r in range(spans)]
                cos_parts = [b[:slots] for b in blocks]
                sin_parts = [b[slots:] for b in blocks]
                cos_half, sin_half = [], []
                for freq in range(spans // 2 + 1):
                    cos_half.append(span_transform(cos_parts, freq, spans))
                    sin_half.append(span_transform(sin_parts, freq, spans))
                held = []
                for freq in range(spans):
                    low = min(freq, spans - freq)
                    c_re, c_im = cos_half[low]
                    s_re, s_im = sin_half[low]
                    if c_im is None:
                        c_im, s_im = jnp.zeros_like(c_re), jnp.zeros_like(s_re)
                    elif low != freq:
                        c_im, s_im = -c_im, -s_im
                    t_re = jnp.broadcast_to(twist_ref[0, freq : freq + 1, at : at + LANES], c_re.shape)
                    t_im = jnp.broadcast_to(twist_ref[1, freq : freq + 1, at : at + LANES], c_re.shape)
                    pairs = (
                        (jnp.where(mark, c_re, c_re - s_im), jnp.where(mark, c_im, c_im + s_re)),
                        (jnp.where(mark, s_re, c_re + s_im), jnp.where(mark, s_im, c_im - s_re)),
                    )
                    held.append(
                        [(re * t_re - im * t_im, re * t_im + im * t_re) for re, im in pairs]
                    )
                    if freq % 2 == 1:
                        row = (freq - 1) * slots
                        for side in range(2):
                            for part in range(2):
                                v_ref[
                                    side * own_rows + row : side * own_rows + row + 2 * slots,
                                    part * count + at : part * count + at + LANES,
                                ] = jnp.concatenate(
                                    [held[0][side][part], held[1][side][part]], axis=0
                                ).astype(v_ref.dtype)
                        held = []

    res = jnp.dot(v_ref[...], tab_ref[...], preferred_element_type=jnp.float32)
    res = res.astype(o_ref.dtype)
    for dest in range(o_ref.shape[0]):
        for side in range(2):
            o_ref[dest, side] = res[
                side * own_rows : (side + 1) * own_rows, dest * LANES : (dest + 1) * LANES
            ]


def position_transform(got, mark, twist, table, spans, hids, slots):
    count = table.shape[1]
    share = count // spans
    team = spans * hids
    rows = spans * slots
    if hids == 2 and share == LANES and slots % 8 == 0 and spans % 2 == 0:
        dests = 4 if spans % 4 == 0 else 2
        out = pl.pallas_call(
            functools.partial(position_kernel, spans, hids, slots),
            grid=(spans // dests,),
            in_specs=[
                pl.BlockSpec(got.shape, lambda i: (0, 0, 0)),
                pl.BlockSpec(mark.shape, lambda i: (0, 0)),
                pl.BlockSpec(twist.shape, lambda i: (0, 0, 0)),
                pl.BlockSpec((2 * count, dests * LANES), lambda i: (0, i)),
            ],
            out_specs=pl.BlockSpec((dests, hids, rows, LANES), lambda i: (i, 0, 0, 0)),
            out_shape=jax.ShapeDtypeStruct((spans, hids, rows, LANES), jnp.bfloat16),
            scratch_shapes=[pltpu.VMEM((2 * rows, 2 * count), jnp.bfloat16)],
            compiler_params=pltpu.CompilerParams(vmem_limit_bytes=58 << 20),
            cost_estimate=pl.CostEstimate(
                flops=2 * 2 * rows * 2 * count * count, bytes_accessed=6 << 20, transcendentals=0
            ),
            name="position_transform",
        )(got, mark, twist, table)
        return out.reshape(team, rows, share)
    wide = got.astype(jnp.float32).reshape(spans, hids, 2, slots, count // hids)
    wide = wide.transpose(2, 0, 3, 1, 4).reshape(2, spans, slots, count)
    ids = jnp.arange(spans, dtype=jnp.int32)
    cos_s, sin_s = turn(ids[:, None] * ids[None], spans)
    exact = lax.Precision.HIGHEST
    re = jnp.einsum("kr,crsn->cksn", cos_s, wide, precision=exact)
    im = jnp.einsum("kr,crsn->cksn", sin_s, wide, precision=exact)
    special = mark > 0.5
    v_re = jnp.stack([jnp.where(special, re[0], re[0] - im[1]), jnp.where(special, re[1], re[0] + im[1])])
    v_im = jnp.stack([jnp.where(special, im[0], im[0] + re[1]), jnp.where(special, im[1], im[0] - re[1])])
    t_re, t_im = twist[0][:, None], twist[1][:, None]
    both = jnp.concatenate([v_re * t_re - v_im * t_im, v_re * t_im + v_im * t_re], axis=-1)
    res = jnp.dot(
        both.astype(jnp.bfloat16).reshape(2 * rows, 2 * count), table, preferred_element_type=jnp.float32
    ).astype(jnp.bfloat16)
    res = res.reshape(2, rows, spans, share).transpose(2, 0, 1, 3)
    res = jnp.repeat(res, hids // 2, axis=1)
    return res.reshape(team, rows, share)


def finish_kernel(spans, slots, back_ref, pick_ref, own_ref, o_ref, held_ref):
    team = back_ref.shape[0]
    groups = held_ref.shape[0]
    for freq in range(spans):
        rows = slice(freq * slots, (freq + 1) * slots)
        block = jnp.concatenate(
            [back_ref[s].astype(jnp.float32)[rows] for s in range(team)], axis=0
        ).astype(jnp.bfloat16)
        value = lax.dot_general(
            block, pick_ref[...], (((0,), (0,)), ((), ())), preferred_element_type=jnp.float32
        )
        for g in range(groups):
            held_ref[g, pl.ds(freq, LANES, stride=spans), :] = value[:, g * LANES : (g + 1) * LANES]
    for g in range(groups):
        lanes = slice(g * LANES, (g + 1) * LANES)
        o_ref[:, lanes] = own_ref[:, lanes] + held_ref[g]


def finish(back, pick, own, spans, slots):
    team, rows, share = back.shape
    if share == LANES and slots % 8 == 0 and own.shape[1] % LANES == 0:
        return pl.pallas_call(
            functools.partial(finish_kernel, spans, slots),
            out_shape=jax.ShapeDtypeStruct(own.shape, jnp.float32),
            scratch_shapes=[pltpu.VMEM((own.shape[1] // LANES, own.shape[0], LANES), jnp.float32)],
            compiler_params=pltpu.CompilerParams(vmem_limit_bytes=48 << 20),
            cost_estimate=pl.CostEstimate(
                flops=2 * own.shape[0] * pick.size, bytes_accessed=5 << 20, transcendentals=0
            ),
            name="finish",
        )(back, pick, own)
    value = jnp.einsum(
        "skjn,sjm->nkm",
        back.reshape(team, spans, slots, share),
        pick.reshape(team, slots, pick.shape[1]),
        preferred_element_type=jnp.float32,
    )
    return own + value.reshape(own.shape)


def ffn_norm_kernel(z_ref, up_ref, gain_ref, grad_ref, low_ref):
    grad = norm_backward(z_ref[...], gain_ref[...], up_ref[...].astype(jnp.float32))
    low = grad.astype(jnp.bfloat16)
    grad_ref[...] = grad
    low_ref[...] = low


def ffn_norm(z_ffn, grad_out, gain):
    rows, width = z_ffn.shape
    tile = pl.BlockSpec((ROWS, width), lambda i: (i, 0))
    return pl.pallas_call(
        ffn_norm_kernel,
        grid=(rows // ROWS,),
        in_specs=[tile, tile, pl.BlockSpec((1, width), lambda i: (0, 0))],
        out_specs=[tile, tile],
        out_shape=[
            jax.ShapeDtypeStruct(z_ffn.shape, jnp.float32),
            jax.ShapeDtypeStruct(z_ffn.shape, jnp.bfloat16),
        ],
        compiler_params=pltpu.CompilerParams(vmem_limit_bytes=32 << 20),
        cost_estimate=SMALL,
        name="ffn_norm",
    )(z_ffn, grad_out, gain[None])


def mix_norm_kernel(z_ref, gain_ref, order_ref, core_ref):
    normed = (norm_parts(z_ref[...])[0] * gain_ref[...]).astype(jnp.bfloat16)
    core_ref[...] = jnp.dot(normed, order_ref[...], preferred_element_type=jnp.float32).astype(jnp.bfloat16)


def mix_norm(z_mix, gain, order):
    rows, width = z_mix.shape
    tile = pl.BlockSpec((ROWS, width), lambda i: (i, 0))
    return pl.pallas_call(
        mix_norm_kernel,
        grid=(rows // ROWS,),
        in_specs=[tile, pl.BlockSpec((1, width), lambda i: (0, 0)), pl.BlockSpec(order.shape, lambda i: (0, 0))],
        out_specs=tile,
        out_shape=jax.ShapeDtypeStruct(z_mix.shape, jnp.bfloat16),
        compiler_params=pltpu.CompilerParams(vmem_limit_bytes=32 << 20),
        cost_estimate=SMALL,
        name="mix_norm",
    )(z_mix, gain[None], order)


def gelu_slope(values):
    scale = math.sqrt(2.0 / math.pi)
    a = values.astype(jnp.float32)
    square = a * a
    tanh = jnp.tanh(scale * a * (1.0 + 0.044715 * square))
    upper = 0.5 * (1.0 + tanh)
    return upper + (0.5 * scale) * a * (1.0 - tanh * tanh) * (1.0 + (3.0 * 0.044715) * square)


def slope_kernel(where_ref, pre_act_ref, slope_ref):
    slope_ref[...] = gelu_slope(pre_act_ref[...])


def slope_rows(where, pre_act, rows, step):
    hids, units = lax.axis_size("hid"), pre_act.shape[1]
    steps = rows // ROWS
    return pl.pallas_call(
        slope_kernel,
        grid_spec=pltpu.PrefetchScalarGridSpec(
            num_scalar_prefetch=1,
            grid=(steps,),
            in_specs=[pl.BlockSpec((ROWS, units), lambda i, w: (lax.rem(w[0] + step, hids) * steps + i, 0))],
            out_specs=pl.BlockSpec((ROWS, units), lambda i, w: (i, 0)),
        ),
        out_shape=jax.ShapeDtypeStruct((rows, units), jnp.float32),
        compiler_params=pltpu.CompilerParams(vmem_limit_bytes=32 << 20),
        cost_estimate=SMALL,
        name="slope_rows",
    )(where, pre_act)


def mix_kernel(count, hids, where_ref, z_ref, ffn_ref, gain_ref, tab_ref, *refs):
    parts, (mix_ref, spec_ref) = refs[:count], refs[count:]
    summed = parts[0][...].astype(jnp.float32)
    for part in parts[1:]:
        summed += part[...].astype(jnp.float32)
    mix = norm_backward(z_ref[...], gain_ref[...], ffn_ref[...] + summed)
    low = mix.astype(jnp.bfloat16)
    mix_ref[...] = low
    spec_ref[...] = lax.dot_general(
        tab_ref[...], low, (((1,), (1,)), ((), ())), preferred_element_type=jnp.float32
    ).astype(jnp.bfloat16)


def mix_rows(where, z_mix, ffn_grad, gain, table, parts, hids):
    rows, width = parts[0].shape
    size = min(rows, 256)
    steps = rows // size
    tile = pl.BlockSpec((size, width), lambda i, w: (i, 0))
    own = pl.BlockSpec((size, width), lambda i, w: (w[0] * steps + i, 0))
    return pl.pallas_call(
        functools.partial(mix_kernel, len(parts), hids),
        grid_spec=pltpu.PrefetchScalarGridSpec(
            num_scalar_prefetch=1,
            grid=(steps,),
            in_specs=[
                own,
                own,
                pl.BlockSpec((1, width), lambda i, w: (0, 0)),
                pl.BlockSpec(table.shape, lambda i, w: (0, 0)),
                *[tile for _ in parts],
            ],
            out_specs=[tile, pl.BlockSpec((table.shape[0], size), lambda i, w: (0, i))],
        ),
        out_shape=[
            jax.ShapeDtypeStruct((rows, width), jnp.bfloat16),
            jax.ShapeDtypeStruct((table.shape[0], rows), jnp.bfloat16),
        ],
        compiler_params=pltpu.CompilerParams(vmem_limit_bytes=32 << 20),
        cost_estimate=SMALL,
        name="mix_rows",
    )(where, z_mix, ffn_grad, gain[None], table, *parts)


def weight_pieces(w_out, w_in, first, during):
    chips, cores, groups = (lax.axis_size(name) for name in ("seq", "sub", "groups"))
    mine = [w_out, w_in]
    if groups == 2:
        mine = [jnp.where(lax.axis_index("groups") == 0, w_out, w_in)]
    near = [((0, 0), (w_out, w_in))]
    steps = sorted(range(1, chips), key=lambda d: (min(d, chips - d), d))
    waves = [steps[k : k + 2] for k in range(0, len(steps), 2)]
    arrived = []
    for wave in waves:
        if arrived:
            mine = lax.optimization_barrier((tuple(mine), arrived[-1], first))[0]
        came = [tuple(lax.ppermute(w, "seq", shift_pairs(chips, d)) for w in mine) for d in wave]
        held = [i for i, ((d, k), _) in enumerate(near) if k == 1]
        if held:
            came, ready, during = lax.optimization_barrier((came, [near[i][1] for i in held], during))
            for i, arrays in zip(held, ready):
                near[i] = (near[i][0], arrays)
        arrived.append([x for blocks in came for x in blocks])
        for d, blocks in zip(wave, came):
            near.append(((d, 0), blocks))
            if groups == 2:
                near.append(((d, 1), (lax.ppermute(blocks[0], "groups", shift_pairs(2, 1)),)))
    pieces = [((0, d, k), arrays) for (d, k), arrays in near]
    for e in range(1, cores):
        for (d, k), arrays in near:
            pieces.append(
                ((e, d, k), tuple(lax.ppermute(x, "sub", shift_pairs(cores, -e)) for x in arrays))
            )
    return pieces, arrived, during


def piece_rows(key, width, shard, seq, sub, group, chips, cores):
    e, d, k = key
    row = (lax.rem(seq + chips - d, chips) * cores + lax.rem(sub + e, cores)) * shard
    if d and lax.axis_size("groups") == 2:
        return [row + lax.rem(group + k, 2) * width]
    return [row, row + width]


def feed_kernel(keys, count, shard, chips, cores, carried, ready, where_ref, x_ref, pre_act_ref, *refs):
    blocks, refs = list(refs[:count]), refs[count + carried :]
    pre_ref, part_ref, weights, total = refs
    width = x_ref.shape[1]
    for key in keys:
        for at in piece_rows(key, width, shard, where_ref[1], where_ref[2], where_ref[3], chips, cores):
            weights[pl.ds(pl.multiple_of(at, shard), shard), :] = blocks.pop(0)[...]
    act_grad = jnp.dot(x_ref[...], weights[:width, :], preferred_element_type=jnp.float32)
    slope = pre_act_ref[...] if ready else gelu_slope(pre_act_ref[...])
    pre_grad = (slope * act_grad).astype(jnp.bfloat16)
    pre_ref[...] = pre_grad
    term = lax.dot_general(
        pre_grad, weights[width:, :], (((1,), (1,)), ((), ())), preferred_element_type=jnp.float32
    )
    first = pl.program_id(0) == 0

    @pl.when(first)
    def _():
        total[...] = term

    @pl.when(jnp.logical_not(first))
    def _():
        total[...] += term

    @pl.when(pl.program_id(0) == pl.num_programs(0) - 1)
    def _():
        part_ref[...] = total[...].astype(part_ref.dtype)


def feed_rows(where, low, pre_act, pieces, rows, step, carried, slope=None):
    chips, cores, hids = (lax.axis_size(name) for name in ("seq", "sub", "hid"))
    width, units = low.shape[1], pre_act.shape[1]
    shard = pieces[0][1][0].shape[0]
    tile = 768 if units % 768 == 0 else 128
    keys = [key for key, _ in pieces]
    flat = [x for _, arrays in pieces for x in arrays]

    def row_block(i, where_ref):
        return (lax.rem(where_ref[0] + step, hids), i)

    extra = [] if carried is None else [carried]
    return pl.pallas_call(
        functools.partial(feed_kernel, keys, len(flat), shard, chips, cores, len(extra), slope is not None),
        grid_spec=pltpu.PrefetchScalarGridSpec(
            num_scalar_prefetch=1,
            grid=(units // tile,),
            in_specs=[
                pl.BlockSpec((rows, width), lambda i, w: (lax.rem(w[0] + step, hids), 0)),
                pl.BlockSpec((rows, tile), row_block if slope is None else lambda i, w: (0, i)),
                *[pl.BlockSpec((x.shape[0], tile), lambda i, w: (0, i)) for x in flat],
                *[pl.BlockSpec(memory_space=pl.ANY) for _ in extra],
            ],
            out_specs=[
                pl.BlockSpec((rows, tile), row_block),
                pl.BlockSpec((rows, width), lambda i, w: (0, 0)),
            ],
            scratch_shapes=[
                pltpu.VMEM((2 * width, tile), jnp.bfloat16),
                pltpu.VMEM((rows, width), jnp.float32),
            ],
        ),
        out_shape=[
            jax.ShapeDtypeStruct(pre_act.shape, jnp.bfloat16),
            jax.ShapeDtypeStruct((rows, width), jnp.bfloat16),
        ],
        input_output_aliases={3 + len(flat): 0} if extra else {},
        compiler_params=pltpu.CompilerParams(vmem_limit_bytes=48 << 20),
        cost_estimate=SMALL,
        name="feed_rows",
    )(where, low, pre_act if slope is None else slope, *flat, *extra)


def whole_weights(pieces, width):
    chips, cores = lax.axis_size("seq"), lax.axis_size("sub")
    shard, units = pieces[0][1][0].shape
    places = [lax.axis_index(name) for name in ("seq", "sub", "groups")]
    whole = jnp.zeros((2 * width, units), jnp.bfloat16)
    for key, arrays in pieces:
        for at, x in zip(piece_rows(key, width, shard, *places, chips, cores), arrays):
            whole = lax.dynamic_update_slice_in_dim(whole, x, at, 0)
    return whole


def local(z_mix, z_ffn, pre_act, grad_out, gain_mix, gain_ffn, w_in, w_out):
    tok_rows, width = z_mix.shape
    unit_count = pre_act.shape[1]
    hids = lax.axis_size("hid")
    hid_index = lax.axis_index("hid")
    cores = lax.axis_size("sub")
    chips = lax.axis_size("seq")
    spans = chips * cores
    team = spans * hids
    half = width // 2
    slots = -(-half // team)
    rows = tok_rows // hids
    col_count = width // hids
    seq_length = tok_rows * spans
    shard_rows = w_in.shape[0]
    bf16 = jnp.bfloat16
    contract_units = (((1,), (1,)), ((), ()))
    contract_rows = (((0,), (0,)), ((), ()))

    def row_part(values, index):
        return lax.dynamic_slice_in_dim(values, index * rows, rows, 0)

    where = jnp.stack([lax.axis_index(name) for name in ("hid", "seq", "sub", "groups")])

    feats = jnp.arange(width, dtype=jnp.int32)
    core_ids = (lax.axis_index("sub") + jnp.arange(cores, dtype=jnp.int32)) % cores
    core_order = (
        jnp.arange(chips, dtype=jnp.int32)[None, :, None] * cores + core_ids[:, None, None]
    ) * shard_rows + jnp.arange(shard_rows, dtype=jnp.int32)[None, None]
    core_reorder = (feats[:, None] == core_order.reshape(1, width)).astype(bf16)

    ffn_grad, ffn_low = ffn_norm(z_ffn, grad_out, gain_ffn)
    fast = shard_rows % 16 == 0 and rows % ROWS == 0 and unit_count % 128 == 0
    pieces, arrived, normed_core = weight_pieces(
        w_out, w_in, (ffn_low,), mix_norm(z_mix, gain_mix, core_reorder)
    )

    def core_rows(left, right, core):
        part = left[:, core * (width // cores) : (core + 1) * (width // cores)]
        return lax.dot_general(part, right, contract_rows, preferred_element_type=jnp.float32)

    def others_rows(left, right):
        return [core_rows(left, right, core).astype(bf16) for core in range(1, cores)]

    def chip_sum(left, right, sent):
        total = core_rows(left, right, 0)
        for core, part in enumerate(sent, 1):
            total += lax.ppermute(part, "sub", shift_pairs(cores, core)).astype(jnp.float32)
        return total.astype(bf16)

    def over_chips(total):
        return lax.psum_scatter(total, "seq", scatter_dimension=0, tiled=True).astype(jnp.float32)

    activation = lax.optimization_barrier(gelu_tanh(pre_act.astype(jnp.float32)).astype(bf16))
    total_out = lax.dot_general(ffn_low, activation, contract_rows, preferred_element_type=jnp.float32)
    total_out, *_ = lax.optimization_barrier((total_out.astype(bf16), *arrived[-1]))
    grad_w_out = lax.psum_scatter(total_out, SPANS, scatter_dimension=0, tiled=True).astype(jnp.float32)
    partials = []
    if fast:
        pre_grad = None
        for step in [*range(1, hids), 0]:
            pre_grad, part = feed_rows(where, ffn_low, pre_act, pieces, rows, step, pre_grad)
            partials.append(part)
    else:
        whole = whole_weights(pieces, width)
        act_grad = jnp.dot(ffn_low, whole[:width], preferred_element_type=jnp.float32)
        pre_grad = (gelu_slope(pre_act) * act_grad).astype(bf16)
        product = lax.dot_general(
            pre_grad, whole[width:], contract_units, preferred_element_type=jnp.float32
        ).astype(bf16)
        for step in [*range(1, hids), 0]:
            partials.append(row_part(product, (hid_index + step) % hids))

    seed = jnp.zeros((), jnp.int32)
    seed, *_ = lax.optimization_barrier((seed, *partials[:-1]))
    feat_tab = lax.optimization_barrier(feature_table(feats + seed, seed, width, slots, team))

    parts = [partials.pop()]
    for step, part in enumerate(partials, 1):
        parts.append(lax.ppermute(part, "hid", shift_pairs(hids, step)))
    sent = others_rows(normed_core, pre_grad)
    feat_tab, *_ = lax.optimization_barrier((feat_tab, *sent))
    mix_low, spectral = mix_rows(where, z_mix, ffn_grad, gain_mix, feat_tab, parts, hids)

    pre_grad, seed, spectral = lax.optimization_barrier((pre_grad, seed, spectral))
    grad_w_in = over_chips(chip_sum(normed_core, pre_grad, sent))
    pos_tab = lax.optimization_barrier(position_table(tok_rows, seed))
    t_cos, t_sin = turn(
        (jnp.arange(spans, dtype=jnp.int32) + seed)[:, None] * (jnp.arange(tok_rows, dtype=jnp.int32) + seed)[None],
        seq_length,
    )
    twist = jnp.stack([t_cos, t_sin]) * (1.0 / math.sqrt(seq_length * width))
    team_index = lax.axis_index(TEAM)
    mark = ((team_index * slots + jnp.arange(slots, dtype=jnp.int32)) == seed).astype(jnp.float32)[:, None]
    own_ids = hid_index * col_count + jnp.arange(col_count, dtype=jnp.int32) + seed
    own_slot = jnp.where(own_ids < half, own_ids, jnp.where(own_ids == half, 0, width - own_ids))
    pick = (jnp.arange(team * slots, dtype=jnp.int32)[:, None] == own_slot[None]).astype(bf16)

    got = lax.all_to_all(
        spectral.reshape(team, 2 * slots, rows), TEAM, split_axis=0, concat_axis=0, tiled=True
    )
    def col_part(values, index):
        return lax.dynamic_slice_in_dim(values, index * col_count, col_count, 1)

    own = jnp.zeros((tok_rows, col_count), bf16)
    own = lax.dynamic_update_slice_in_dim(own, col_part(mix_low, hid_index), hid_index * rows, 0)
    for step in range(1, hids):
        sent = col_part(mix_low, (hid_index + step) % hids)
        came = lax.ppermute(sent, "hid", shift_pairs(hids, step))
        own = lax.dynamic_update_slice_in_dim(own, came, (hid_index - step) % hids * rows, 0)
    got, own, grad_w_out = lax.optimization_barrier((got, own, grad_w_out))
    sent_back = position_transform(got, mark, twist, pos_tab, spans, hids, slots)
    back = lax.all_to_all(sent_back, TEAM, split_axis=0, concat_axis=0, tiled=True)
    back, grad_w_in, grad_w_out = lax.optimization_barrier((back, grad_w_in, grad_w_out))
    grad_in = finish(back, pick, own, spans, slots)
    return (grad_in, grad_w_in, grad_w_out)


def solution(mesh):
    in_specs = (
        P(("groups", "seq", "sub"), None),
        P(("groups", "seq", "sub"), None),
        P(("groups", "seq", "sub"), "hid"),
        P(("groups", "seq", "sub"), None),
        P(),
        P(),
        P(("seq", "sub"), "hid"),
        P(("seq", "sub"), "hid"),
    )
    out_specs = (
        P(("groups", "seq", "sub"), "hid"),
        P(("groups", "seq", "sub"), "hid"),
        P(("groups", "seq", "sub"), "hid"),
    )
    return jax.shard_map(local, mesh=mesh, in_specs=in_specs, out_specs=out_specs, check_vma=False)
```

```python
import functools
import math

import jax
import jax.numpy as jnp
from jax import lax
from jax.experimental import pallas as pl
from jax.experimental.pallas import tpu as pltpu
from jax.sharding import PartitionSpec as P

epsilon = 1e-05
SPANS = ("seq", "sub")
TEAM = ("seq", "sub", "hid")
LANES = 128
ROWS = 128
SMALL = pl.CostEstimate(flops=1 << 20, bytes_accessed=1 << 16, transcendentals=0)


def norm_parts(values):
    values = values.astype(jnp.float32)
    row_mean = jnp.mean(values, axis=-1, keepdims=True)
    centred = values - row_mean
    inv_std = lax.rsqrt(jnp.mean(centred * centred, axis=-1, keepdims=True) + epsilon)
    return (centred * inv_std, inv_std)


def norm_backward(values, gain_vec, upstream):
    unit_rows, inv_std = norm_parts(values)
    scaled = upstream * gain_vec
    return inv_std * (
        scaled
        - jnp.mean(scaled, axis=-1, keepdims=True)
        - unit_rows * jnp.mean(scaled * unit_rows, axis=-1, keepdims=True)
    )


def gelu_tanh(values):
    return jax.nn.gelu(values, approximate=True)


def shift_pairs(size, step):
    return [(i, (i + step) % size) for i in range(size)]


def turn(products, period):
    angles = (2.0 * math.pi / period) * (products % period).astype(jnp.float32)
    return (jnp.cos(angles), jnp.sin(angles))


def feature_table(feats, seed, width, slots, team):
    half = width // 2
    cos_a, sin_a = turn(slots * (jnp.arange(team, dtype=jnp.int32) + seed)[:, None] * feats[None], width)
    cos_b, sin_b = turn((jnp.arange(slots, dtype=jnp.int32) + seed)[:, None] * feats[None], width)
    slot = lax.broadcasted_iota(jnp.int32, (team, slots, 1), 0) * slots
    slot = slot + lax.broadcasted_iota(jnp.int32, (team, slots, 1), 1)
    cos_all = cos_a[:, None] * cos_b[None] - sin_a[:, None] * sin_b[None]
    sin_all = sin_a[:, None] * cos_b[None] + cos_a[:, None] * sin_b[None]
    top = (1 - 2 * (feats % 2)).astype(jnp.float32)[None, None]
    sin_all = jnp.where(slot == 0, top, sin_all)
    table = jnp.where(slot < half, jnp.stack([cos_all, sin_all], axis=1).transpose(1, 0, 2, 3), 0.0)
    return table.astype(jnp.bfloat16).transpose(1, 0, 2, 3).reshape(team * 2 * slots, width)


def position_table(count, seed):
    fine = 32
    coarse = count // fine
    col = jnp.arange(count, dtype=jnp.int32) + seed
    cos_a, sin_a = turn(fine * (jnp.arange(coarse, dtype=jnp.int32) + seed)[:, None] * col[None], count)
    cos_b, sin_b = turn((jnp.arange(fine, dtype=jnp.int32) + seed)[:, None] * col[None], count)
    cos_a, sin_a = cos_a[:, None], sin_a[:, None]
    cos_b, sin_b = cos_b[None], sin_b[None]
    both = jnp.stack([cos_a * cos_b - sin_a * sin_b, -sin_a * cos_b - cos_a * sin_b])
    return both.astype(jnp.bfloat16).reshape(2 * count, count)


def combine(terms):
    total = None
    for factor, value in terms:
        if abs(factor) < 1e-12:
            continue
        if abs(factor - 1.0) < 1e-12:
            total = value if total is None else total + value
        elif abs(factor + 1.0) < 1e-12:
            total = -value if total is None else total - value
        else:
            part = factor * value
            total = part if total is None else total + part
    return total


def span_transform(parts, freq, spans):
    angles = [2.0 * math.pi * (r * freq % spans) / spans for r in range(spans)]
    real = combine([(math.cos(a), p) for a, p in zip(angles, parts)])
    imag = combine([(math.sin(a), p) for a, p in zip(angles, parts)])
    return (real, imag)


def position_kernel(spans, hids, slots, x_ref, mark_ref, twist_ref, tab_ref, o_ref, v_ref):
    rows_in = x_ref.shape[2]
    count = rows_in * hids
    own_rows = spans * slots

    @pl.when(pl.program_id(0) == 0)
    def _():
        mark = jnp.broadcast_to(mark_ref[...], (slots, LANES)) > 0.5
        for hid in range(hids):
            for piece in range(rows_in // LANES):
                lanes = slice(piece * LANES, (piece + 1) * LANES)
                at = hid * rows_in + piece * LANES
                blocks = [x_ref[r * hids + hid, :, lanes].astype(jnp.float32) for r in range(spans)]
                cos_parts = [b[:slots] for b in blocks]
                sin_parts = [b[slots:] for b in blocks]
                cos_half, sin_half = [], []
                for freq in range(spans // 2 + 1):
                    cos_half.append(span_transform(cos_parts, freq, spans))
                    sin_half.append(span_transform(sin_parts, freq, spans))
                held = []
                for freq in range(spans):
                    low = min(freq, spans - freq)
                    c_re, c_im = cos_half[low]
                    s_re, s_im = sin_half[low]
                    if c_im is None:
                        c_im, s_im = jnp.zeros_like(c_re), jnp.zeros_like(s_re)
                    elif low != freq:
                        c_im, s_im = -c_im, -s_im
                    t_re = jnp.broadcast_to(twist_ref[0, freq : freq + 1, at : at + LANES], c_re.shape)
                    t_im = jnp.broadcast_to(twist_ref[1, freq : freq + 1, at : at + LANES], c_re.shape)
                    pairs = (
                        (jnp.where(mark, c_re, c_re - s_im), jnp.where(mark, c_im, c_im + s_re)),
                        (jnp.where(mark, s_re, c_re + s_im), jnp.where(mark, s_im, c_im - s_re)),
                    )
                    held.append(
                        [(re * t_re - im * t_im, re * t_im + im * t_re) for re, im in pairs]
                    )
                    if freq % 2 == 1:
                        row = (freq - 1) * slots
                        for side in range(2):
                            for part in range(2):
                                v_ref[
                                    side * own_rows + row : side * own_rows + row + 2 * slots,
                                    part * count + at : part * count + at + LANES,
                                ] = jnp.concatenate(
                                    [held[0][side][part], held[1][side][part]], axis=0
                                ).astype(v_ref.dtype)
                        held = []

    res = jnp.dot(v_ref[...], tab_ref[...], preferred_element_type=jnp.float32)
    res = res.astype(o_ref.dtype)
    for dest in range(o_ref.shape[0]):
        for side in range(2):
            o_ref[dest, side] = res[
                side * own_rows : (side + 1) * own_rows, dest * LANES : (dest + 1) * LANES
            ]


def position_transform(got, mark, twist, table, spans, hids, slots):
    count = table.shape[1]
    share = count // spans
    team = spans * hids
    rows = spans * slots
    if hids == 2 and share == LANES and slots % 8 == 0 and spans % 2 == 0:
        dests = 4 if spans % 4 == 0 else 2
        out = pl.pallas_call(
            functools.partial(position_kernel, spans, hids, slots),
            grid=(spans // dests,),
            in_specs=[
                pl.BlockSpec(got.shape, lambda i: (0, 0, 0)),
                pl.BlockSpec(mark.shape, lambda i: (0, 0)),
                pl.BlockSpec(twist.shape, lambda i: (0, 0, 0)),
                pl.BlockSpec((2 * count, dests * LANES), lambda i: (0, i)),
            ],
            out_specs=pl.BlockSpec((dests, hids, rows, LANES), lambda i: (i, 0, 0, 0)),
            out_shape=jax.ShapeDtypeStruct((spans, hids, rows, LANES), jnp.bfloat16),
            scratch_shapes=[pltpu.VMEM((2 * rows, 2 * count), jnp.bfloat16)],
            compiler_params=pltpu.CompilerParams(vmem_limit_bytes=58 << 20),
            cost_estimate=pl.CostEstimate(
                flops=2 * 2 * rows * 2 * count * count, bytes_accessed=6 << 20, transcendentals=0
            ),
            name="position_transform",
        )(got, mark, twist, table)
        return out.reshape(team, rows, share)
    wide = got.astype(jnp.float32).reshape(spans, hids, 2, slots, count // hids)
    wide = wide.transpose(2, 0, 3, 1, 4).reshape(2, spans, slots, count)
    ids = jnp.arange(spans, dtype=jnp.int32)
    cos_s, sin_s = turn(ids[:, None] * ids[None], spans)
    exact = lax.Precision.HIGHEST
    re = jnp.einsum("kr,crsn->cksn", cos_s, wide, precision=exact)
    im = jnp.einsum("kr,crsn->cksn", sin_s, wide, precision=exact)
    special = mark > 0.5
    v_re = jnp.stack([jnp.where(special, re[0], re[0] - im[1]), jnp.where(special, re[1], re[0] + im[1])])
    v_im = jnp.stack([jnp.where(special, im[0], im[0] + re[1]), jnp.where(special, im[1], im[0] - re[1])])
    t_re, t_im = twist[0][:, None], twist[1][:, None]
    both = jnp.concatenate([v_re * t_re - v_im * t_im, v_re * t_im + v_im * t_re], axis=-1)
    res = jnp.dot(
        both.astype(jnp.bfloat16).reshape(2 * rows, 2 * count), table, preferred_element_type=jnp.float32
    ).astype(jnp.bfloat16)
    res = res.reshape(2, rows, spans, share).transpose(2, 0, 1, 3)
    res = jnp.repeat(res, hids // 2, axis=1)
    return res.reshape(team, rows, share)


def finish_kernel(spans, slots, back_ref, pick_ref, own_ref, o_ref, held_ref):
    team = back_ref.shape[0]
    groups = held_ref.shape[0]
    for freq in range(spans):
        rows = slice(freq * slots, (freq + 1) * slots)
        block = jnp.concatenate(
            [back_ref[s].astype(jnp.float32)[rows] for s in range(team)], axis=0
        ).astype(jnp.bfloat16)
        value = lax.dot_general(
            block, pick_ref[...], (((0,), (0,)), ((), ())), preferred_element_type=jnp.float32
        )
        for g in range(groups):
            held_ref[g, pl.ds(freq, LANES, stride=spans), :] = value[:, g * LANES : (g + 1) * LANES]
    for g in range(groups):
        lanes = slice(g * LANES, (g + 1) * LANES)
        o_ref[:, lanes] = own_ref[:, lanes] + held_ref[g]


def finish(back, pick, own, spans, slots):
    team, rows, share = back.shape
    if share == LANES and slots % 8 == 0 and own.shape[1] % LANES == 0:
        return pl.pallas_call(
            functools.partial(finish_kernel, spans, slots),
            out_shape=jax.ShapeDtypeStruct(own.shape, jnp.float32),
            scratch_shapes=[pltpu.VMEM((own.shape[1] // LANES, own.shape[0], LANES), jnp.float32)],
            compiler_params=pltpu.CompilerParams(vmem_limit_bytes=48 << 20),
            cost_estimate=pl.CostEstimate(
                flops=2 * own.shape[0] * pick.size, bytes_accessed=5 << 20, transcendentals=0
            ),
            name="finish",
        )(back, pick, own)
    value = jnp.einsum(
        "skjn,sjm->nkm",
        back.reshape(team, spans, slots, share),
        pick.reshape(team, slots, pick.shape[1]),
        preferred_element_type=jnp.float32,
    )
    return own + value.reshape(own.shape)


def ffn_norm_kernel(z_ref, up_ref, gain_ref, grad_ref, low_ref):
    grad = norm_backward(z_ref[...], gain_ref[...], up_ref[...].astype(jnp.float32))
    low = grad.astype(jnp.bfloat16)
    grad_ref[...] = grad
    low_ref[...] = low


def ffn_norm(z_ffn, grad_out, gain):
    rows, width = z_ffn.shape
    tile = pl.BlockSpec((ROWS, width), lambda i: (i, 0))
    return pl.pallas_call(
        ffn_norm_kernel,
        grid=(rows // ROWS,),
        in_specs=[tile, tile, pl.BlockSpec((1, width), lambda i: (0, 0))],
        out_specs=[tile, tile],
        out_shape=[
            jax.ShapeDtypeStruct(z_ffn.shape, jnp.float32),
            jax.ShapeDtypeStruct(z_ffn.shape, jnp.bfloat16),
        ],
        compiler_params=pltpu.CompilerParams(vmem_limit_bytes=32 << 20),
        cost_estimate=SMALL,
        name="ffn_norm",
    )(z_ffn, grad_out, gain[None])


def mix_norm_kernel(z_ref, gain_ref, order_ref, core_ref):
    normed = (norm_parts(z_ref[...])[0] * gain_ref[...]).astype(jnp.bfloat16)
    core_ref[...] = jnp.dot(normed, order_ref[...], preferred_element_type=jnp.float32).astype(jnp.bfloat16)


def mix_norm(z_mix, gain, order):
    rows, width = z_mix.shape
    tile = pl.BlockSpec((ROWS, width), lambda i: (i, 0))
    return pl.pallas_call(
        mix_norm_kernel,
        grid=(rows // ROWS,),
        in_specs=[tile, pl.BlockSpec((1, width), lambda i: (0, 0)), pl.BlockSpec(order.shape, lambda i: (0, 0))],
        out_specs=tile,
        out_shape=jax.ShapeDtypeStruct(z_mix.shape, jnp.bfloat16),
        compiler_params=pltpu.CompilerParams(vmem_limit_bytes=32 << 20),
        cost_estimate=SMALL,
        name="mix_norm",
    )(z_mix, gain[None], order)


def gelu_slope(values):
    scale = math.sqrt(2.0 / math.pi)
    a = values.astype(jnp.float32)
    square = a * a
    tanh = jnp.tanh(scale * a * (1.0 + 0.044715 * square))
    upper = 0.5 * (1.0 + tanh)
    return upper + (0.5 * scale) * a * (1.0 - tanh * tanh) * (1.0 + (3.0 * 0.044715) * square)


def slope_kernel(where_ref, pre_act_ref, slope_ref):
    slope_ref[...] = gelu_slope(pre_act_ref[...])


def slope_rows(where, pre_act, rows, step):
    hids, units = lax.axis_size("hid"), pre_act.shape[1]
    steps = rows // ROWS
    return pl.pallas_call(
        slope_kernel,
        grid_spec=pltpu.PrefetchScalarGridSpec(
            num_scalar_prefetch=1,
            grid=(steps,),
            in_specs=[pl.BlockSpec((ROWS, units), lambda i, w: (lax.rem(w[0] + step, hids) * steps + i, 0))],
            out_specs=pl.BlockSpec((ROWS, units), lambda i, w: (i, 0)),
        ),
        out_shape=jax.ShapeDtypeStruct((rows, units), jnp.float32),
        compiler_params=pltpu.CompilerParams(vmem_limit_bytes=32 << 20),
        cost_estimate=SMALL,
        name="slope_rows",
    )(where, pre_act)


def mix_kernel(count, hids, where_ref, z_ref, ffn_ref, gain_ref, tab_ref, *refs):
    parts, (mix_ref, spec_ref) = refs[:count], refs[count:]
    summed = parts[0][...].astype(jnp.float32)
    for part in parts[1:]:
        summed += part[...].astype(jnp.float32)
    mix = norm_backward(z_ref[...], gain_ref[...], ffn_ref[...] + summed)
    low = mix.astype(jnp.bfloat16)
    mix_ref[...] = low
    spec_ref[...] = lax.dot_general(
        tab_ref[...], low, (((1,), (1,)), ((), ())), preferred_element_type=jnp.float32
    ).astype(jnp.bfloat16)


def mix_rows(where, z_mix, ffn_grad, gain, table, parts, hids):
    rows, width = parts[0].shape
    size = min(rows, 512)
    steps = rows // size
    tile = pl.BlockSpec((size, width), lambda i, w: (i, 0))
    own = pl.BlockSpec((size, width), lambda i, w: (w[0] * steps + i, 0))
    return pl.pallas_call(
        functools.partial(mix_kernel, len(parts), hids),
        grid_spec=pltpu.PrefetchScalarGridSpec(
            num_scalar_prefetch=1,
            grid=(steps,),
            in_specs=[
                own,
                own,
                pl.BlockSpec((1, width), lambda i, w: (0, 0)),
                pl.BlockSpec(table.shape, lambda i, w: (0, 0)),
                *[tile for _ in parts],
            ],
            out_specs=[tile, pl.BlockSpec((table.shape[0], size), lambda i, w: (0, i))],
        ),
        out_shape=[
            jax.ShapeDtypeStruct((rows, width), jnp.bfloat16),
            jax.ShapeDtypeStruct((table.shape[0], rows), jnp.bfloat16),
        ],
        compiler_params=pltpu.CompilerParams(vmem_limit_bytes=32 << 20),
        cost_estimate=SMALL,
        name="mix_rows",
    )(where, z_mix, ffn_grad, gain[None], table, *parts)


def weight_pieces(w_out, w_in, first, during):
    chips, cores, groups = (lax.axis_size(name) for name in ("seq", "sub", "groups"))
    mine = [w_out, w_in]
    if groups == 2:
        mine = [jnp.where(lax.axis_index("groups") == 0, w_out, w_in)]
    near = [((0, 0), (w_out, w_in))]
    steps = sorted(range(1, chips), key=lambda d: (min(d, chips - d), d))
    waves = [steps[k : k + 2] for k in range(0, len(steps), 2)]
    arrived = []
    for wave in waves:
        if arrived:
            mine = lax.optimization_barrier((tuple(mine), arrived[-1], first))[0]
        came = [tuple(lax.ppermute(w, "seq", shift_pairs(chips, d)) for w in mine) for d in wave]
        held = [i for i, ((d, k), _) in enumerate(near) if k == 1]
        if held:
            came, ready, during = lax.optimization_barrier((came, [near[i][1] for i in held], during))
            for i, arrays in zip(held, ready):
                near[i] = (near[i][0], arrays)
        arrived.append([x for blocks in came for x in blocks])
        for d, blocks in zip(wave, came):
            near.append(((d, 0), blocks))
            if groups == 2:
                near.append(((d, 1), (lax.ppermute(blocks[0], "groups", shift_pairs(2, 1)),)))
    pieces = [((0, d, k), arrays) for (d, k), arrays in near]
    for e in range(1, cores):
        for (d, k), arrays in near:
            pieces.append(
                ((e, d, k), tuple(lax.ppermute(x, "sub", shift_pairs(cores, -e)) for x in arrays))
            )
    return pieces, arrived, during


def piece_rows(key, width, shard, seq, sub, group, chips, cores):
    e, d, k = key
    row = (lax.rem(seq + chips - d, chips) * cores + lax.rem(sub + e, cores)) * shard
    if d and lax.axis_size("groups") == 2:
        return [row + lax.rem(group + k, 2) * width]
    return [row, row + width]


def feed_kernel(keys, count, shard, chips, cores, carried, ready, where_ref, x_ref, pre_act_ref, *refs):
    blocks, refs = list(refs[:count]), refs[count + carried :]
    pre_ref, part_ref, weights, total = refs
    width = x_ref.shape[1]
    for key in keys:
        for at in piece_rows(key, width, shard, where_ref[1], where_ref[2], where_ref[3], chips, cores):
            weights[pl.ds(pl.multiple_of(at, shard), shard), :] = blocks.pop(0)[...]
    act_grad = jnp.dot(x_ref[...], weights[:width, :], preferred_element_type=jnp.float32)
    slope = pre_act_ref[...] if ready else gelu_slope(pre_act_ref[...])
    pre_grad = (slope * act_grad).astype(jnp.bfloat16)
    pre_ref[...] = pre_grad
    term = lax.dot_general(
        pre_grad, weights[width:, :], (((1,), (1,)), ((), ())), preferred_element_type=jnp.float32
    )
    first = pl.program_id(0) == 0

    @pl.when(first)
    def _():
        total[...] = term

    @pl.when(jnp.logical_not(first))
    def _():
        total[...] += term

    @pl.when(pl.program_id(0) == pl.num_programs(0) - 1)
    def _():
        part_ref[...] = total[...].astype(part_ref.dtype)


def feed_rows(where, low, pre_act, pieces, rows, step, carried, slope=None):
    chips, cores, hids = (lax.axis_size(name) for name in ("seq", "sub", "hid"))
    width, units = low.shape[1], pre_act.shape[1]
    shard = pieces[0][1][0].shape[0]
    tile = 768 if units % 768 == 0 else 128
    keys = [key for key, _ in pieces]
    flat = [x for _, arrays in pieces for x in arrays]

    def row_block(i, where_ref):
        return (lax.rem(where_ref[0] + step, hids), i)

    extra = [] if carried is None else [carried]
    return pl.pallas_call(
        functools.partial(feed_kernel, keys, len(flat), shard, chips, cores, len(extra), slope is not None),
        grid_spec=pltpu.PrefetchScalarGridSpec(
            num_scalar_prefetch=1,
            grid=(units // tile,),
            in_specs=[
                pl.BlockSpec((rows, width), lambda i, w: (lax.rem(w[0] + step, hids), 0)),
                pl.BlockSpec((rows, tile), row_block if slope is None else lambda i, w: (0, i)),
                *[pl.BlockSpec((x.shape[0], tile), lambda i, w: (0, i)) for x in flat],
                *[pl.BlockSpec(memory_space=pl.ANY) for _ in extra],
            ],
            out_specs=[
                pl.BlockSpec((rows, tile), row_block),
                pl.BlockSpec((rows, width), lambda i, w: (0, 0)),
            ],
            scratch_shapes=[
                pltpu.VMEM((2 * width, tile), jnp.bfloat16),
                pltpu.VMEM((rows, width), jnp.float32),
            ],
        ),
        out_shape=[
            jax.ShapeDtypeStruct(pre_act.shape, jnp.bfloat16),
            jax.ShapeDtypeStruct((rows, width), jnp.bfloat16),
        ],
        input_output_aliases={3 + len(flat): 0} if extra else {},
        compiler_params=pltpu.CompilerParams(vmem_limit_bytes=48 << 20),
        cost_estimate=SMALL,
        name="feed_rows",
    )(where, low, pre_act if slope is None else slope, *flat, *extra)


def whole_weights(pieces, width):
    chips, cores = lax.axis_size("seq"), lax.axis_size("sub")
    shard, units = pieces[0][1][0].shape
    places = [lax.axis_index(name) for name in ("seq", "sub", "groups")]
    whole = jnp.zeros((2 * width, units), jnp.bfloat16)
    for key, arrays in pieces:
        for at, x in zip(piece_rows(key, width, shard, *places, chips, cores), arrays):
            whole = lax.dynamic_update_slice_in_dim(whole, x, at, 0)
    return whole


def local(z_mix, z_ffn, pre_act, grad_out, gain_mix, gain_ffn, w_in, w_out):
    tok_rows, width = z_mix.shape
    unit_count = pre_act.shape[1]
    hids = lax.axis_size("hid")
    hid_index = lax.axis_index("hid")
    cores = lax.axis_size("sub")
    chips = lax.axis_size("seq")
    spans = chips * cores
    team = spans * hids
    half = width // 2
    slots = -(-half // team)
    rows = tok_rows // hids
    col_count = width // hids
    seq_length = tok_rows * spans
    shard_rows = w_in.shape[0]
    bf16 = jnp.bfloat16
    contract_units = (((1,), (1,)), ((), ()))
    contract_rows = (((0,), (0,)), ((), ()))

    def row_part(values, index):
        return lax.dynamic_slice_in_dim(values, index * rows, rows, 0)

    where = jnp.stack([lax.axis_index(name) for name in ("hid", "seq", "sub", "groups")])

    feats = jnp.arange(width, dtype=jnp.int32)
    core_ids = (lax.axis_index("sub") + jnp.arange(cores, dtype=jnp.int32)) % cores
    core_order = (
        jnp.arange(chips, dtype=jnp.int32)[None, :, None] * cores + core_ids[:, None, None]
    ) * shard_rows + jnp.arange(shard_rows, dtype=jnp.int32)[None, None]
    core_reorder = (feats[:, None] == core_order.reshape(1, width)).astype(bf16)

    ffn_grad, ffn_low = ffn_norm(z_ffn, grad_out, gain_ffn)
    fast = shard_rows % 16 == 0 and rows % ROWS == 0 and unit_count % 128 == 0
    pieces, arrived, normed_core = weight_pieces(
        w_out, w_in, (ffn_low,), mix_norm(z_mix, gain_mix, core_reorder)
    )

    def core_rows(left, right, core):
        part = left[:, core * (width // cores) : (core + 1) * (width // cores)]
        return lax.dot_general(part, right, contract_rows, preferred_element_type=jnp.float32)

    def others_rows(left, right):
        return [core_rows(left, right, core).astype(bf16) for core in range(1, cores)]

    def chip_sum(left, right, sent):
        total = core_rows(left, right, 0)
        for core, part in enumerate(sent, 1):
            total += lax.ppermute(part, "sub", shift_pairs(cores, core)).astype(jnp.float32)
        return total.astype(bf16)

    def over_chips(total):
        return lax.psum_scatter(total, "seq", scatter_dimension=0, tiled=True).astype(jnp.float32)

    activation = lax.optimization_barrier(gelu_tanh(pre_act.astype(jnp.float32)).astype(bf16))
    total_out = lax.dot_general(ffn_low, activation, contract_rows, preferred_element_type=jnp.float32)
    total_out, *_ = lax.optimization_barrier((total_out.astype(bf16), *arrived[-1]))
    grad_w_out = lax.psum_scatter(total_out, SPANS, scatter_dimension=0, tiled=True).astype(jnp.float32)
    partials = []
    if fast:
        pre_grad = None
        for step in [*range(1, hids), 0]:
            pre_grad, part = feed_rows(where, ffn_low, pre_act, pieces, rows, step, pre_grad)
            partials.append(part)
    else:
        whole = whole_weights(pieces, width)
        act_grad = jnp.dot(ffn_low, whole[:width], preferred_element_type=jnp.float32)
        pre_grad = (gelu_slope(pre_act) * act_grad).astype(bf16)
        product = lax.dot_general(
            pre_grad, whole[width:], contract_units, preferred_element_type=jnp.float32
        ).astype(bf16)
        for step in [*range(1, hids), 0]:
            partials.append(row_part(product, (hid_index + step) % hids))

    seed = jnp.zeros((), jnp.int32)
    seed, *_ = lax.optimization_barrier((seed, *partials[:-1]))
    feat_tab = lax.optimization_barrier(feature_table(feats + seed, seed, width, slots, team))

    parts = [partials.pop()]
    for step, part in enumerate(partials, 1):
        parts.append(lax.ppermute(part, "hid", shift_pairs(hids, step)))
    sent = others_rows(normed_core, pre_grad)
    feat_tab, *_ = lax.optimization_barrier((feat_tab, *sent))
    mix_low, spectral = mix_rows(where, z_mix, ffn_grad, gain_mix, feat_tab, parts, hids)

    pre_grad, seed, spectral = lax.optimization_barrier((pre_grad, seed, spectral))
    grad_w_in = over_chips(chip_sum(normed_core, pre_grad, sent))
    pos_tab = lax.optimization_barrier(position_table(tok_rows, seed))
    t_cos, t_sin = turn(
        (jnp.arange(spans, dtype=jnp.int32) + seed)[:, None] * (jnp.arange(tok_rows, dtype=jnp.int32) + seed)[None],
        seq_length,
    )
    twist = jnp.stack([t_cos, t_sin]) * (1.0 / math.sqrt(seq_length * width))
    team_index = lax.axis_index(TEAM)
    mark = ((team_index * slots + jnp.arange(slots, dtype=jnp.int32)) == seed).astype(jnp.float32)[:, None]
    own_ids = hid_index * col_count + jnp.arange(col_count, dtype=jnp.int32) + seed
    own_slot = jnp.where(own_ids < half, own_ids, jnp.where(own_ids == half, 0, width - own_ids))
    pick = (jnp.arange(team * slots, dtype=jnp.int32)[:, None] == own_slot[None]).astype(bf16)

    got = lax.all_to_all(
        spectral.reshape(team, 2 * slots, rows), TEAM, split_axis=0, concat_axis=0, tiled=True
    )
    def col_part(values, index):
        return lax.dynamic_slice_in_dim(values, index * col_count, col_count, 1)

    own = jnp.zeros((tok_rows, col_count), bf16)
    own = lax.dynamic_update_slice_in_dim(own, col_part(mix_low, hid_index), hid_index * rows, 0)
    for step in range(1, hids):
        sent = col_part(mix_low, (hid_index + step) % hids)
        came = lax.ppermute(sent, "hid", shift_pairs(hids, step))
        own = lax.dynamic_update_slice_in_dim(own, came, (hid_index - step) % hids * rows, 0)
    got, own, grad_w_out = lax.optimization_barrier((got, own, grad_w_out))
    sent_back = position_transform(got, mark, twist, pos_tab, spans, hids, slots)
    back = lax.all_to_all(sent_back, TEAM, split_axis=0, concat_axis=0, tiled=True)
    back, grad_w_in, grad_w_out = lax.optimization_barrier((back, grad_w_in, grad_w_out))
    grad_in = finish(back, pick, own, spans, slots)
    return (grad_in, grad_w_in, grad_w_out)


def solution(mesh):
    in_specs = (
        P(("groups", "seq", "sub"), None),
        P(("groups", "seq", "sub"), None),
        P(("groups", "seq", "sub"), "hid"),
        P(("groups", "seq", "sub"), None),
        P(),
        P(),
        P(("seq", "sub"), "hid"),
        P(("seq", "sub"), "hid"),
    )
    out_specs = (
        P(("groups", "seq", "sub"), "hid"),
        P(("groups", "seq", "sub"), "hid"),
        P(("groups", "seq", "sub"), "hid"),
    )
    return jax.shard_map(local, mesh=mesh, in_specs=in_specs, out_specs=out_specs, check_vma=False)
```

```python
import functools
import math

import jax
import jax.numpy as jnp
from jax import lax
from jax.experimental import pallas as pl
from jax.experimental.pallas import tpu as pltpu
from jax.sharding import PartitionSpec as P

epsilon = 1e-05
SPANS = ("seq", "sub")
TEAM = ("seq", "sub", "hid")
LANES = 128
ROWS = 256
SMALL = pl.CostEstimate(flops=1 << 20, bytes_accessed=1 << 16, transcendentals=0)


def norm_parts(values):
    values = values.astype(jnp.float32)
    row_mean = jnp.mean(values, axis=-1, keepdims=True)
    centred = values - row_mean
    inv_std = lax.rsqrt(jnp.mean(centred * centred, axis=-1, keepdims=True) + epsilon)
    return (centred * inv_std, inv_std)


def norm_backward(values, gain_vec, upstream):
    unit_rows, inv_std = norm_parts(values)
    scaled = upstream * gain_vec
    return inv_std * (
        scaled
        - jnp.mean(scaled, axis=-1, keepdims=True)
        - unit_rows * jnp.mean(scaled * unit_rows, axis=-1, keepdims=True)
    )


def gelu_tanh(values):
    return jax.nn.gelu(values, approximate=True)


def shift_pairs(size, step):
    return [(i, (i + step) % size) for i in range(size)]


def turn(products, period):
    angles = (2.0 * math.pi / period) * (products % period).astype(jnp.float32)
    return (jnp.cos(angles), jnp.sin(angles))


def feature_table(feats, seed, width, slots, team):
    half = width // 2
    cos_a, sin_a = turn(slots * (jnp.arange(team, dtype=jnp.int32) + seed)[:, None] * feats[None], width)
    cos_b, sin_b = turn((jnp.arange(slots, dtype=jnp.int32) + seed)[:, None] * feats[None], width)
    slot = lax.broadcasted_iota(jnp.int32, (team, slots, 1), 0) * slots
    slot = slot + lax.broadcasted_iota(jnp.int32, (team, slots, 1), 1)
    cos_all = cos_a[:, None] * cos_b[None] - sin_a[:, None] * sin_b[None]
    sin_all = sin_a[:, None] * cos_b[None] + cos_a[:, None] * sin_b[None]
    top = (1 - 2 * (feats % 2)).astype(jnp.float32)[None, None]
    sin_all = jnp.where(slot == 0, top, sin_all)
    table = jnp.where(slot < half, jnp.stack([cos_all, sin_all], axis=1).transpose(1, 0, 2, 3), 0.0)
    return table.astype(jnp.bfloat16).transpose(1, 0, 2, 3).reshape(team * 2 * slots, width)


def position_table(count, seed):
    fine = 32
    coarse = count // fine
    col = jnp.arange(count, dtype=jnp.int32) + seed
    cos_a, sin_a = turn(fine * (jnp.arange(coarse, dtype=jnp.int32) + seed)[:, None] * col[None], count)
    cos_b, sin_b = turn((jnp.arange(fine, dtype=jnp.int32) + seed)[:, None] * col[None], count)
    cos_a, sin_a = cos_a[:, None], sin_a[:, None]
    cos_b, sin_b = cos_b[None], sin_b[None]
    both = jnp.stack([cos_a * cos_b - sin_a * sin_b, -sin_a * cos_b - cos_a * sin_b])
    return both.astype(jnp.bfloat16).reshape(2 * count, count)


def combine(terms):
    total = None
    for factor, value in terms:
        if abs(factor) < 1e-12:
            continue
        if abs(factor - 1.0) < 1e-12:
            total = value if total is None else total + value
        elif abs(factor + 1.0) < 1e-12:
            total = -value if total is None else total - value
        else:
            part = factor * value
            total = part if total is None else total + part
    return total


def span_transform(parts, freq, spans):
    angles = [2.0 * math.pi * (r * freq % spans) / spans for r in range(spans)]
    real = combine([(math.cos(a), p) for a, p in zip(angles, parts)])
    imag = combine([(math.sin(a), p) for a, p in zip(angles, parts)])
    return (real, imag)


def position_kernel(spans, hids, slots, x_ref, mark_ref, twist_ref, tab_ref, o_ref, v_ref):
    rows_in = x_ref.shape[2]
    count = rows_in * hids
    own_rows = spans * slots

    @pl.when(pl.program_id(0) == 0)
    def _():
        mark = jnp.broadcast_to(mark_ref[...], (slots, LANES)) > 0.5
        for hid in range(hids):
            for piece in range(rows_in // LANES):
                lanes = slice(piece * LANES, (piece + 1) * LANES)
                at = hid * rows_in + piece * LANES
                blocks = [x_ref[r * hids + hid, :, lanes].astype(jnp.float32) for r in range(spans)]
                cos_parts = [b[:slots] for b in blocks]
                sin_parts = [b[slots:] for b in blocks]
                cos_half, sin_half = [], []
                for freq in range(spans // 2 + 1):
                    cos_half.append(span_transform(cos_parts, freq, spans))
                    sin_half.append(span_transform(sin_parts, freq, spans))
                held = []
                for freq in range(spans):
                    low = min(freq, spans - freq)
                    c_re, c_im = cos_half[low]
                    s_re, s_im = sin_half[low]
                    if c_im is None:
                        c_im, s_im = jnp.zeros_like(c_re), jnp.zeros_like(s_re)
                    elif low != freq:
                        c_im, s_im = -c_im, -s_im
                    t_re = jnp.broadcast_to(twist_ref[0, freq : freq + 1, at : at + LANES], c_re.shape)
                    t_im = jnp.broadcast_to(twist_ref[1, freq : freq + 1, at : at + LANES], c_re.shape)
                    pairs = (
                        (jnp.where(mark, c_re, c_re - s_im), jnp.where(mark, c_im, c_im + s_re)),
                        (jnp.where(mark, s_re, c_re + s_im), jnp.where(mark, s_im, c_im - s_re)),
                    )
                    held.append(
                        [(re * t_re - im * t_im, re * t_im + im * t_re) for re, im in pairs]
                    )
                    if freq % 2 == 1:
                        row = (freq - 1) * slots
                        for side in range(2):
                            for part in range(2):
                                v_ref[
                                    side * own_rows + row : side * own_rows + row + 2 * slots,
                                    part * count + at : part * count + at + LANES,
                                ] = jnp.concatenate(
                                    [held[0][side][part], held[1][side][part]], axis=0
                                ).astype(v_ref.dtype)
                        held = []

    res = jnp.dot(v_ref[...], tab_ref[...], preferred_element_type=jnp.float32)
    res = res.astype(o_ref.dtype)
    for dest in range(o_ref.shape[0]):
        for side in range(2):
            o_ref[dest, side] = res[
                side * own_rows : (side + 1) * own_rows, dest * LANES : (dest + 1) * LANES
            ]


def position_transform(got, mark, twist, table, spans, hids, slots):
    count = table.shape[1]
    share = count // spans
    team = spans * hids
    rows = spans * slots
    if hids == 2 and share == LANES and slots % 8 == 0 and spans % 2 == 0:
        dests = 4 if spans % 4 == 0 else 2
        out = pl.pallas_call(
            functools.partial(position_kernel, spans, hids, slots),
            grid=(spans // dests,),
            in_specs=[
                pl.BlockSpec(got.shape, lambda i: (0, 0, 0)),
                pl.BlockSpec(mark.shape, lambda i: (0, 0)),
                pl.BlockSpec(twist.shape, lambda i: (0, 0, 0)),
                pl.BlockSpec((2 * count, dests * LANES), lambda i: (0, i)),
            ],
            out_specs=pl.BlockSpec((dests, hids, rows, LANES), lambda i: (i, 0, 0, 0)),
            out_shape=jax.ShapeDtypeStruct((spans, hids, rows, LANES), jnp.bfloat16),
            scratch_shapes=[pltpu.VMEM((2 * rows, 2 * count), jnp.bfloat16)],
            compiler_params=pltpu.CompilerParams(vmem_limit_bytes=58 << 20),
            cost_estimate=pl.CostEstimate(
                flops=2 * 2 * rows * 2 * count * count, bytes_accessed=6 << 20, transcendentals=0
            ),
            name="position_transform",
        )(got, mark, twist, table)
        return out.reshape(team, rows, share)
    wide = got.astype(jnp.float32).reshape(spans, hids, 2, slots, count // hids)
    wide = wide.transpose(2, 0, 3, 1, 4).reshape(2, spans, slots, count)
    ids = jnp.arange(spans, dtype=jnp.int32)
    cos_s, sin_s = turn(ids[:, None] * ids[None], spans)
    exact = lax.Precision.HIGHEST
    re = jnp.einsum("kr,crsn->cksn", cos_s, wide, precision=exact)
    im = jnp.einsum("kr,crsn->cksn", sin_s, wide, precision=exact)
    special = mark > 0.5
    v_re = jnp.stack([jnp.where(special, re[0], re[0] - im[1]), jnp.where(special, re[1], re[0] + im[1])])
    v_im = jnp.stack([jnp.where(special, im[0], im[0] + re[1]), jnp.where(special, im[1], im[0] - re[1])])
    t_re, t_im = twist[0][:, None], twist[1][:, None]
    both = jnp.concatenate([v_re * t_re - v_im * t_im, v_re * t_im + v_im * t_re], axis=-1)
    res = jnp.dot(
        both.astype(jnp.bfloat16).reshape(2 * rows, 2 * count), table, preferred_element_type=jnp.float32
    ).astype(jnp.bfloat16)
    res = res.reshape(2, rows, spans, share).transpose(2, 0, 1, 3)
    res = jnp.repeat(res, hids // 2, axis=1)
    return res.reshape(team, rows, share)


def finish_kernel(spans, slots, back_ref, pick_ref, own_ref, o_ref, held_ref):
    team = back_ref.shape[0]
    groups = held_ref.shape[0]
    for freq in range(spans):
        rows = slice(freq * slots, (freq + 1) * slots)
        block = jnp.concatenate(
            [back_ref[s].astype(jnp.float32)[rows] for s in range(team)], axis=0
        ).astype(jnp.bfloat16)
        value = lax.dot_general(
            block, pick_ref[...], (((0,), (0,)), ((), ())), preferred_element_type=jnp.float32
        )
        for g in range(groups):
            held_ref[g, pl.ds(freq, LANES, stride=spans), :] = value[:, g * LANES : (g + 1) * LANES]
    for g in range(groups):
        lanes = slice(g * LANES, (g + 1) * LANES)
        o_ref[:, lanes] = own_ref[:, lanes] + held_ref[g]


def finish(back, pick, own, spans, slots):
    team, rows, share = back.shape
    if share == LANES and slots % 8 == 0 and own.shape[1] % LANES == 0:
        return pl.pallas_call(
            functools.partial(finish_kernel, spans, slots),
            out_shape=jax.ShapeDtypeStruct(own.shape, jnp.float32),
            scratch_shapes=[pltpu.VMEM((own.shape[1] // LANES, own.shape[0], LANES), jnp.float32)],
            compiler_params=pltpu.CompilerParams(vmem_limit_bytes=48 << 20),
            cost_estimate=pl.CostEstimate(
                flops=2 * own.shape[0] * pick.size, bytes_accessed=5 << 20, transcendentals=0
            ),
            name="finish",
        )(back, pick, own)
    value = jnp.einsum(
        "skjn,sjm->nkm",
        back.reshape(team, spans, slots, share),
        pick.reshape(team, slots, pick.shape[1]),
        preferred_element_type=jnp.float32,
    )
    return own + value.reshape(own.shape)


def ffn_norm_kernel(z_ref, up_ref, gain_ref, grad_ref, low_ref):
    grad = norm_backward(z_ref[...], gain_ref[...], up_ref[...].astype(jnp.float32))
    low = grad.astype(jnp.bfloat16)
    grad_ref[...] = grad
    low_ref[...] = low


def ffn_norm(z_ffn, grad_out, gain):
    rows, width = z_ffn.shape
    tile = pl.BlockSpec((ROWS, width), lambda i: (i, 0))
    return pl.pallas_call(
        ffn_norm_kernel,
        grid=(rows // ROWS,),
        in_specs=[tile, tile, pl.BlockSpec((1, width), lambda i: (0, 0))],
        out_specs=[tile, tile],
        out_shape=[
            jax.ShapeDtypeStruct(z_ffn.shape, jnp.float32),
            jax.ShapeDtypeStruct(z_ffn.shape, jnp.bfloat16),
        ],
        compiler_params=pltpu.CompilerParams(vmem_limit_bytes=32 << 20),
        cost_estimate=SMALL,
        name="ffn_norm",
    )(z_ffn, grad_out, gain[None])


def mix_norm_kernel(z_ref, gain_ref, order_ref, core_ref):
    normed = (norm_parts(z_ref[...])[0] * gain_ref[...]).astype(jnp.bfloat16)
    core_ref[...] = jnp.dot(normed, order_ref[...], preferred_element_type=jnp.float32).astype(jnp.bfloat16)


def mix_norm(z_mix, gain, order):
    rows, width = z_mix.shape
    tile = pl.BlockSpec((ROWS, width), lambda i: (i, 0))
    return pl.pallas_call(
        mix_norm_kernel,
        grid=(rows // ROWS,),
        in_specs=[tile, pl.BlockSpec((1, width), lambda i: (0, 0)), pl.BlockSpec(order.shape, lambda i: (0, 0))],
        out_specs=tile,
        out_shape=jax.ShapeDtypeStruct(z_mix.shape, jnp.bfloat16),
        compiler_params=pltpu.CompilerParams(vmem_limit_bytes=32 << 20),
        cost_estimate=SMALL,
        name="mix_norm",
    )(z_mix, gain[None], order)


def gelu_slope(values):
    scale = math.sqrt(2.0 / math.pi)
    a = values.astype(jnp.float32)
    square = a * a
    tanh = jnp.tanh(scale * a * (1.0 + 0.044715 * square))
    upper = 0.5 * (1.0 + tanh)
    return upper + (0.5 * scale) * a * (1.0 - tanh * tanh) * (1.0 + (3.0 * 0.044715) * square)


def slope_kernel(where_ref, pre_act_ref, slope_ref):
    slope_ref[...] = gelu_slope(pre_act_ref[...])


def slope_rows(where, pre_act, rows, step):
    hids, units = lax.axis_size("hid"), pre_act.shape[1]
    steps = rows // ROWS
    return pl.pallas_call(
        slope_kernel,
        grid_spec=pltpu.PrefetchScalarGridSpec(
            num_scalar_prefetch=1,
            grid=(steps,),
            in_specs=[pl.BlockSpec((ROWS, units), lambda i, w: (lax.rem(w[0] + step, hids) * steps + i, 0))],
            out_specs=pl.BlockSpec((ROWS, units), lambda i, w: (i, 0)),
        ),
        out_shape=jax.ShapeDtypeStruct((rows, units), jnp.float32),
        compiler_params=pltpu.CompilerParams(vmem_limit_bytes=32 << 20),
        cost_estimate=SMALL,
        name="slope_rows",
    )(where, pre_act)


def mix_kernel(count, hids, where_ref, z_ref, ffn_ref, gain_ref, tab_ref, *refs):
    parts, (mix_ref, spec_ref) = refs[:count], refs[count:]
    summed = parts[0][...].astype(jnp.float32)
    for part in parts[1:]:
        summed += part[...].astype(jnp.float32)
    mix = norm_backward(z_ref[...], gain_ref[...], ffn_ref[...] + summed)
    low = mix.astype(jnp.bfloat16)
    mix_ref[...] = low
    spec_ref[...] = lax.dot_general(
        tab_ref[...], low, (((1,), (1,)), ((), ())), preferred_element_type=jnp.float32
    ).astype(jnp.bfloat16)


def mix_rows(where, z_mix, ffn_grad, gain, table, parts, hids):
    rows, width = parts[0].shape
    size = min(rows, 512)
    steps = rows // size
    tile = pl.BlockSpec((size, width), lambda i, w: (i, 0))
    own = pl.BlockSpec((size, width), lambda i, w: (w[0] * steps + i, 0))
    return pl.pallas_call(
        functools.partial(mix_kernel, len(parts), hids),
        grid_spec=pltpu.PrefetchScalarGridSpec(
            num_scalar_prefetch=1,
            grid=(steps,),
            in_specs=[
                own,
                own,
                pl.BlockSpec((1, width), lambda i, w: (0, 0)),
                pl.BlockSpec(table.shape, lambda i, w: (0, 0)),
                *[tile for _ in parts],
            ],
            out_specs=[tile, pl.BlockSpec((table.shape[0], size), lambda i, w: (0, i))],
        ),
        out_shape=[
            jax.ShapeDtypeStruct((rows, width), jnp.bfloat16),
            jax.ShapeDtypeStruct((table.shape[0], rows), jnp.bfloat16),
        ],
        compiler_params=pltpu.CompilerParams(vmem_limit_bytes=32 << 20),
        cost_estimate=SMALL,
        name="mix_rows",
    )(where, z_mix, ffn_grad, gain[None], table, *parts)


def weight_pieces(w_out, w_in, first, during):
    chips, cores, groups = (lax.axis_size(name) for name in ("seq", "sub", "groups"))
    mine = [w_out, w_in]
    if groups == 2:
        mine = [jnp.where(lax.axis_index("groups") == 0, w_out, w_in)]
    near = [((0, 0), (w_out, w_in))]
    steps = sorted(range(1, chips), key=lambda d: (min(d, chips - d), d))
    waves = [steps[k : k + 2] for k in range(0, len(steps), 2)]
    arrived = []
    for wave in waves:
        if arrived:
            mine = lax.optimization_barrier((tuple(mine), arrived[-1], first))[0]
        came = [tuple(lax.ppermute(w, "seq", shift_pairs(chips, d)) for w in mine) for d in wave]
        held = [i for i, ((d, k), _) in enumerate(near) if k == 1]
        if held:
            came, ready, during = lax.optimization_barrier((came, [near[i][1] for i in held], during))
            for i, arrays in zip(held, ready):
                near[i] = (near[i][0], arrays)
        arrived.append([x for blocks in came for x in blocks])
        for d, blocks in zip(wave, came):
            near.append(((d, 0), blocks))
            if groups == 2:
                near.append(((d, 1), (lax.ppermute(blocks[0], "groups", shift_pairs(2, 1)),)))
    pieces = [((0, d, k), arrays) for (d, k), arrays in near]
    for e in range(1, cores):
        for (d, k), arrays in near:
            pieces.append(
                ((e, d, k), tuple(lax.ppermute(x, "sub", shift_pairs(cores, -e)) for x in arrays))
            )
    return pieces, arrived, during


def piece_rows(key, width, shard, seq, sub, group, chips, cores):
    e, d, k = key
    row = (lax.rem(seq + chips - d, chips) * cores + lax.rem(sub + e, cores)) * shard
    if d and lax.axis_size("groups") == 2:
        return [row + lax.rem(group + k, 2) * width]
    return [row, row + width]


def feed_kernel(keys, count, shard, chips, cores, carried, ready, where_ref, x_ref, pre_act_ref, *refs):
    blocks, refs = list(refs[:count]), refs[count + carried :]
    pre_ref, part_ref, weights, total = refs
    width = x_ref.shape[1]
    for key in keys:
        for at in piece_rows(key, width, shard, where_ref[1], where_ref[2], where_ref[3], chips, cores):
            weights[pl.ds(pl.multiple_of(at, shard), shard), :] = blocks.pop(0)[...]
    act_grad = jnp.dot(x_ref[...], weights[:width, :], preferred_element_type=jnp.float32)
    slope = pre_act_ref[...] if ready else gelu_slope(pre_act_ref[...])
    pre_grad = (slope * act_grad).astype(jnp.bfloat16)
    pre_ref[...] = pre_grad
    term = lax.dot_general(
        pre_grad, weights[width:, :], (((1,), (1,)), ((), ())), preferred_element_type=jnp.float32
    )
    first = pl.program_id(0) == 0

    @pl.when(first)
    def _():
        total[...] = term

    @pl.when(jnp.logical_not(first))
    def _():
        total[...] += term

    @pl.when(pl.program_id(0) == pl.num_programs(0) - 1)
    def _():
        part_ref[...] = total[...].astype(part_ref.dtype)


def feed_rows(where, low, pre_act, pieces, rows, step, carried, slope=None):
    chips, cores, hids = (lax.axis_size(name) for name in ("seq", "sub", "hid"))
    width, units = low.shape[1], pre_act.shape[1]
    shard = pieces[0][1][0].shape[0]
    tile = 768 if units % 768 == 0 else 128
    keys = [key for key, _ in pieces]
    flat = [x for _, arrays in pieces for x in arrays]

    def row_block(i, where_ref):
        return (lax.rem(where_ref[0] + step, hids), i)

    extra = [] if carried is None else [carried]
    return pl.pallas_call(
        functools.partial(feed_kernel, keys, len(flat), shard, chips, cores, len(extra), slope is not None),
        grid_spec=pltpu.PrefetchScalarGridSpec(
            num_scalar_prefetch=1,
            grid=(units // tile,),
            in_specs=[
                pl.BlockSpec((rows, width), lambda i, w: (lax.rem(w[0] + step, hids), 0)),
                pl.BlockSpec((rows, tile), row_block if slope is None else lambda i, w: (0, i)),
                *[pl.BlockSpec((x.shape[0], tile), lambda i, w: (0, i)) for x in flat],
                *[pl.BlockSpec(memory_space=pl.ANY) for _ in extra],
            ],
            out_specs=[
                pl.BlockSpec((rows, tile), row_block),
                pl.BlockSpec((rows, width), lambda i, w: (0, 0)),
            ],
            scratch_shapes=[
                pltpu.VMEM((2 * width, tile), jnp.bfloat16),
                pltpu.VMEM((rows, width), jnp.float32),
            ],
        ),
        out_shape=[
            jax.ShapeDtypeStruct(pre_act.shape, jnp.bfloat16),
            jax.ShapeDtypeStruct((rows, width), jnp.bfloat16),
        ],
        input_output_aliases={3 + len(flat): 0} if extra else {},
        compiler_params=pltpu.CompilerParams(vmem_limit_bytes=48 << 20),
        cost_estimate=SMALL,
        name="feed_rows",
    )(where, low, pre_act if slope is None else slope, *flat, *extra)


def whole_weights(pieces, width):
    chips, cores = lax.axis_size("seq"), lax.axis_size("sub")
    shard, units = pieces[0][1][0].shape
    places = [lax.axis_index(name) for name in ("seq", "sub", "groups")]
    whole = jnp.zeros((2 * width, units), jnp.bfloat16)
    for key, arrays in pieces:
        for at, x in zip(piece_rows(key, width, shard, *places, chips, cores), arrays):
            whole = lax.dynamic_update_slice_in_dim(whole, x, at, 0)
    return whole


def local(z_mix, z_ffn, pre_act, grad_out, gain_mix, gain_ffn, w_in, w_out):
    tok_rows, width = z_mix.shape
    unit_count = pre_act.shape[1]
    hids = lax.axis_size("hid")
    hid_index = lax.axis_index("hid")
    cores = lax.axis_size("sub")
    chips = lax.axis_size("seq")
    spans = chips * cores
    team = spans * hids
    half = width // 2
    slots = -(-half // team)
    rows = tok_rows // hids
    col_count = width // hids
    seq_length = tok_rows * spans
    shard_rows = w_in.shape[0]
    bf16 = jnp.bfloat16
    contract_units = (((1,), (1,)), ((), ()))
    contract_rows = (((0,), (0,)), ((), ()))

    def row_part(values, index):
        return lax.dynamic_slice_in_dim(values, index * rows, rows, 0)

    where = jnp.stack([lax.axis_index(name) for name in ("hid", "seq", "sub", "groups")])

    feats = jnp.arange(width, dtype=jnp.int32)
    core_ids = (lax.axis_index("sub") + jnp.arange(cores, dtype=jnp.int32)) % cores
    core_order = (
        jnp.arange(chips, dtype=jnp.int32)[None, :, None] * cores + core_ids[:, None, None]
    ) * shard_rows + jnp.arange(shard_rows, dtype=jnp.int32)[None, None]
    core_reorder = (feats[:, None] == core_order.reshape(1, width)).astype(bf16)

    ffn_grad, ffn_low = ffn_norm(z_ffn, grad_out, gain_ffn)
    fast = shard_rows % 16 == 0 and rows % ROWS == 0 and unit_count % 128 == 0
    pieces, arrived, normed_core = weight_pieces(
        w_out, w_in, (ffn_low,), mix_norm(z_mix, gain_mix, core_reorder)
    )

    def core_rows(left, right, core):
        part = left[:, core * (width // cores) : (core + 1) * (width // cores)]
        return lax.dot_general(part, right, contract_rows, preferred_element_type=jnp.float32)

    def others_rows(left, right):
        return [core_rows(left, right, core).astype(bf16) for core in range(1, cores)]

    def chip_sum(left, right, sent):
        total = core_rows(left, right, 0)
        for core, part in enumerate(sent, 1):
            total += lax.ppermute(part, "sub", shift_pairs(cores, core)).astype(jnp.float32)
        return total.astype(bf16)

    def over_chips(total):
        return lax.psum_scatter(total, "seq", scatter_dimension=0, tiled=True).astype(jnp.float32)

    activation = lax.optimization_barrier(gelu_tanh(pre_act.astype(jnp.float32)).astype(bf16))
    total_out = lax.dot_general(ffn_low, activation, contract_rows, preferred_element_type=jnp.float32)
    total_out, *_ = lax.optimization_barrier((total_out.astype(bf16), *arrived[-1]))
    grad_w_out = lax.psum_scatter(total_out, SPANS, scatter_dimension=0, tiled=True).astype(jnp.float32)
    partials = []
    if fast:
        pre_grad = None
        for step in [*range(1, hids), 0]:
            pre_grad, part = feed_rows(where, ffn_low, pre_act, pieces, rows, step, pre_grad)
            partials.append(part)
    else:
        whole = whole_weights(pieces, width)
        act_grad = jnp.dot(ffn_low, whole[:width], preferred_element_type=jnp.float32)
        pre_grad = (gelu_slope(pre_act) * act_grad).astype(bf16)
        product = lax.dot_general(
            pre_grad, whole[width:], contract_units, preferred_element_type=jnp.float32
        ).astype(bf16)
        for step in [*range(1, hids), 0]:
            partials.append(row_part(product, (hid_index + step) % hids))

    seed = jnp.zeros((), jnp.int32)
    seed, *_ = lax.optimization_barrier((seed, *partials[:-1]))
    feat_tab = lax.optimization_barrier(feature_table(feats + seed, seed, width, slots, team))

    parts = [partials.pop()]
    for step, part in enumerate(partials, 1):
        parts.append(lax.ppermute(part, "hid", shift_pairs(hids, step)))
    sent = others_rows(normed_core, pre_grad)
    feat_tab, *_ = lax.optimization_barrier((feat_tab, *sent))
    mix_low, spectral = mix_rows(where, z_mix, ffn_grad, gain_mix, feat_tab, parts, hids)

    pre_grad, seed, spectral = lax.optimization_barrier((pre_grad, seed, spectral))
    grad_w_in = over_chips(chip_sum(normed_core, pre_grad, sent))
    pos_tab = lax.optimization_barrier(position_table(tok_rows, seed))
    t_cos, t_sin = turn(
        (jnp.arange(spans, dtype=jnp.int32) + seed)[:, None] * (jnp.arange(tok_rows, dtype=jnp.int32) + seed)[None],
        seq_length,
    )
    twist = jnp.stack([t_cos, t_sin]) * (1.0 / math.sqrt(seq_length * width))
    team_index = lax.axis_index(TEAM)
    mark = ((team_index * slots + jnp.arange(slots, dtype=jnp.int32)) == seed).astype(jnp.float32)[:, None]
    own_ids = hid_index * col_count + jnp.arange(col_count, dtype=jnp.int32) + seed
    own_slot = jnp.where(own_ids < half, own_ids, jnp.where(own_ids == half, 0, width - own_ids))
    pick = (jnp.arange(team * slots, dtype=jnp.int32)[:, None] == own_slot[None]).astype(bf16)

    got = lax.all_to_all(
        spectral.reshape(team, 2 * slots, rows), TEAM, split_axis=0, concat_axis=0, tiled=True
    )
    def col_part(values, index):
        return lax.dynamic_slice_in_dim(values, index * col_count, col_count, 1)

    own = jnp.zeros((tok_rows, col_count), bf16)
    own = lax.dynamic_update_slice_in_dim(own, col_part(mix_low, hid_index), hid_index * rows, 0)
    for step in range(1, hids):
        sent = col_part(mix_low, (hid_index + step) % hids)
        came = lax.ppermute(sent, "hid", shift_pairs(hids, step))
        own = lax.dynamic_update_slice_in_dim(own, came, (hid_index - step) % hids * rows, 0)
    got, own, grad_w_out = lax.optimization_barrier((got, own, grad_w_out))
    sent_back = position_transform(got, mark, twist, pos_tab, spans, hids, slots)
    back = lax.all_to_all(sent_back, TEAM, split_axis=0, concat_axis=0, tiled=True)
    back, grad_w_in, grad_w_out = lax.optimization_barrier((back, grad_w_in, grad_w_out))
    grad_in = finish(back, pick, own, spans, slots)
    return (grad_in, grad_w_in, grad_w_out)


def solution(mesh):
    in_specs = (
        P(("groups", "seq", "sub"), None),
        P(("groups", "seq", "sub"), None),
        P(("groups", "seq", "sub"), "hid"),
        P(("groups", "seq", "sub"), None),
        P(),
        P(),
        P(("seq", "sub"), "hid"),
        P(("seq", "sub"), "hid"),
    )
    out_specs = (
        P(("groups", "seq", "sub"), "hid"),
        P(("groups", "seq", "sub"), "hid"),
        P(("groups", "seq", "sub"), "hid"),
    )
    return jax.shard_map(local, mesh=mesh, in_specs=in_specs, out_specs=out_specs, check_vma=False)
```
